256 devices in a mesh: rows: 16 (over x_hi, z), cols: 4 (over x_lo, core), dp: 4 (over y).
Axes of the slice: x: 4 (x_hi: 2, x_lo: 2; x = x_hi * 2 + x_lo), y: 4, z: 8, core: 2. Of those that a mesh axis runs over, the one named last changes fastest.
Arguments:
- fields: float32 [1024, 64, 384], P(('dp', 'rows'), 'cols'), parts along dimension 0, may hold values from -6 to 6
- logit_scale: float32 [6], replicated, may hold values from 4 to 25
- w_qkv: bfloat16 [384, 1152], replicated, may hold values from -0.3125 to 0.3125
- w_proj: bfloat16 [384, 384], replicated, may hold values from -0.3125 to 0.3125
- w_merge: bfloat16 [1536, 768], P(None, 'cols'), may hold values from -0.15625 to 0.15625
- w_up: bfloat16 [768, 3072], P('rows', 'cols'), may hold values from -0.21875 to 0.21875
- w_down: bfloat16 [3072, 768], P('cols', 'rows'), may hold values from -0.109375 to 0.109375
- cotangent: bfloat16 [512, 32, 768], P(('dp', 'rows'), 'cols'), parts along dimension 0, may hold values from -0.59765625 to 0.59765625
Outputs:
- coarse: float32 [512, 32, 768], P(('dp', 'rows'), 'cols'), parts along dimension 0
- grad_coarse: float32 [512, 32, 768], P(('dp', 'rows'), 'cols'), parts along dimension 0
- grad_up: float32 [768, 12288], P('rows', ('dp', 'cols')), parts along dimension 1
- grad_down: float32 [3072, 3072], P('cols', ('dp', 'rows')), parts along dimension 1
The draws below stay inside these ranges and needn't reach their ends.
There are 4 independent parts, one for each index of `dp`. The reference program is written for one: setup_inputs(seed, part) draws one part's arguments, and reference() takes and returns one part's arrays. A program takes and returns all parts, laid end to end along the dimension named above; an argument that names none is the same for every part. Nothing has to cross between parts.
All inputs are finite; a program needn't handle non-finite values.
Results may differ from the reference program's by a relative error of at most 0.02.
Values may be sent and summed in bfloat16 or wider, within the bound.
No kernel may reach another device: no remote copies, remote signals or barrier semaphores. Data moves between devices by JAX's collectives and lax.ppermute only.
A program may use at most 64 MiB of HBM per device.

```python
import math
import jax
import jax.numpy as jnp
from jax import lax

C3 = 384
C4 = 768
FF4 = 3072
HEADS3 = 6
WIN = 16
NR = 256
NC = 64
N_ROWS = 16


def spiked(array, key, source, target, blocks, factor):
    def block_of(axis_at):
        return (jnp.arange(array.shape[axis_at]) // (array.shape[axis_at] // blocks)).reshape((-1,) + (1,) * (array.ndim - 1 - axis_at))

    near = jax.random.permutation(key, blocks)[block_of(target)]
    far = (block_of(target) + blocks // 2) % blocks
    return jnp.where((block_of(source) == near) | (block_of(source) == far), factor * array, array)


def block_scale(own_key, extent, cuts, least, high):
    level, own = 1.0, jax.random.fold_in(own_key, 6)
    for dim, parts in cuts:
        steps = jnp.exp(jax.random.uniform(jax.random.fold_in(own, dim), (parts,), jnp.float32, least / len(cuts), high / len(cuts)))
        level = level * jnp.repeat(steps, extent[dim] // parts).reshape([-1 if axis == dim else 1 for axis in range(len(extent))])
    return level


def gaussian(own_key, dims, deviation, most, cuts=(), kind=jnp.bfloat16):
    array = jax.random.normal(own_key, dims, jnp.float32) * deviation
    if len(cuts) > 0:
        array = block_scale(own_key, dims, cuts, -0.22, 0.18) * array
    return jnp.clip(array, min=-most, max=most).astype(kind)


def noise_with(key, extent, scale, bound, shards, heavy, dtype=jnp.bfloat16):
    entries = scale * jax.random.normal(key, extent, jnp.float32)
    if shards:
        entries = entries * block_scale(key, extent, shards, -0.22, 0.18)
    return jnp.clip(spiked(entries, jax.random.fold_in(key, 3), *heavy), -bound, bound).astype(dtype)


def setup_inputs(seed: int = 0, part: int = 0) -> dict:
    keys = jax.random.split(jax.random.key(seed), 9)
    part_keys = jax.random.split(jax.random.fold_in(keys[8], part), 9)
    return {
        "fields": gaussian(part_keys[0], (NR, NC, C3), 1.0, 6.0, ((0, 16), (1, 4)), jnp.float32),
        "logit_scale": jnp.clip(jnp.exp(jax.random.uniform(keys[1], (HEADS3,), jnp.float32, math.log(4.0), math.log(25.0))), 4.0, 25.0),
        "w_qkv": gaussian(keys[2], (C3, 3 * C3), C3 ** -0.5, 0.3125),
        "w_proj": gaussian(keys[3], (C3, C3), C3 ** -0.5, 0.3125),
        "w_merge": gaussian(keys[4], (4 * C3, C4), (4 * C3) ** -0.5, 0.15625, ((1, 4),)),
        "w_up": gaussian(keys[5], (C4, FF4), C4 ** -0.5, 0.21875, ((0, 16), (1, 4))),
        "w_down": gaussian(keys[6], (FF4, C4), FF4 ** -0.5, 0.109375, ((0, 4), (1, 16))),
        "cotangent": noise_with(part_keys[7], (NR // 2, NC // 2, C4), 0.1, 0.59765625, ((0, 16), (1, 4)), (0, 2, 16, 2.0)),
    }


eps_norm = 1e-05
eps_unit = 1e-06

def layer_norm(value):
    average = lax.optimization_barrier(jnp.mean(value, axis=-1, keepdims=True))
    centred = value - average
    spread = lax.optimization_barrier(jnp.mean(centred * centred, axis=-1, keepdims=True))
    inverse = lax.rsqrt(spread + eps_norm)
    return (centred * inverse, inverse)

def norm_slope(upstream, normed, inverse):
    first_mean = lax.optimization_barrier(jnp.mean(upstream, axis=-1, keepdims=True))
    second_mean = lax.optimization_barrier(jnp.mean(upstream * normed, axis=-1, keepdims=True))
    return inverse * (upstream - first_mean - normed * second_mean)

def unit_heads(value, head_count):
    shaped = value.reshape(value.shape[:-1] + (head_count, value.shape[-1] // head_count))
    squares = lax.optimization_barrier(jnp.sum(shaped * shaped, axis=-1, keepdims=True))
    return (shaped * lax.rsqrt(squares + eps_unit)).reshape(value.shape)

def windows_of(field_grid, window):
    grid_rows, grid_cols, channels = field_grid.shape
    shaped = field_grid.reshape(grid_rows // window, window, grid_cols // window, window, channels)
    return shaped.transpose(0, 2, 1, 3, 4).reshape(-1, window * window, channels)

def grid_of(blocks, grid_rows, grid_cols, window):
    channels = blocks.shape[-1]
    shaped = blocks.reshape(grid_rows // window, grid_cols // window, window, window, channels)
    return shaped.transpose(0, 2, 1, 3, 4).reshape(grid_rows, grid_cols, channels)

def attend_exact(queries, key_rows, value_rows, logit_scale, head_count):
    number, window_size, channels = queries.shape
    width_head = channels // head_count
    query_heads = queries.astype(jnp.float32).reshape(number, window_size, head_count, width_head)
    key_heads = key_rows.astype(jnp.float32).reshape(number, window_size, head_count, width_head)
    value_heads = value_rows.astype(jnp.float32).reshape(number, window_size, head_count, width_head)
    scores = jnp.einsum('wqhd,wkhd->whqk', query_heads, key_heads) * logit_scale[None, :, None, None]
    weights = jnp.exp(scores)
    weights = (weights / lax.optimization_barrier(jnp.sum(weights, axis=-1, keepdims=True))).astype(jnp.bfloat16)
    mixed_out = jnp.einsum('whqk,wkhd->wqhd', weights.astype(jnp.float32), value_heads)
    return mixed_out.reshape(number, window_size, channels)

def merge_patches(field_grid):
    quarters = (field_grid[0::2, 0::2], field_grid[1::2, 0::2], field_grid[0::2, 1::2], field_grid[1::2, 1::2])
    return jnp.concatenate(quarters, axis=-1)

def exact_gelu(value):
    return jax.nn.gelu(value, approximate=False)

def reference(fields, logit_scale, w_qkv, w_proj, w_merge, w_up, w_down, cotangent):
    offset = WIN // 2
    grid_rows, grid_cols, channels = fields.shape
    head_count = logit_scale.shape[0]
    rolled = jnp.roll(fields, (-offset, -offset), (0, 1)).astype(jnp.bfloat16).reshape(-1, channels)
    projected = jnp.dot(rolled, w_qkv, preferred_element_type=jnp.float32)
    queries = unit_heads(projected[:, :channels], head_count).astype(jnp.bfloat16)
    key_rows = unit_heads(projected[:, channels:2 * channels], head_count).astype(jnp.bfloat16)
    value_rows = projected[:, 2 * channels:].astype(jnp.bfloat16)

    def blocked(flat_rows):
        return windows_of(flat_rows.reshape(grid_rows, grid_cols, channels), WIN)

    def one_window(triple):
        return attend_exact(triple[0][None], triple[1][None], triple[2][None], logit_scale, head_count)[0]
    mixed = lax.map(one_window, (blocked(queries), blocked(key_rows), blocked(value_rows)))
    mixed = grid_of(mixed, grid_rows, grid_cols, WIN)
    mixed = jnp.roll(mixed, (offset, offset), (0, 1)).astype(jnp.bfloat16).reshape(-1, channels)
    branch = jnp.dot(mixed, w_proj, preferred_element_type=jnp.float32)
    normed, _ = layer_norm(branch)
    stream = fields + normed.reshape(fields.shape)
    merged = merge_patches(stream).astype(jnp.bfloat16)
    coarse_rows, coarse_cols = (merged.shape[0], merged.shape[1])
    merged_rows = merged.reshape(-1, merged.shape[-1])
    level, _ = layer_norm(jnp.dot(merged_rows, w_merge, preferred_element_type=jnp.float32))
    level_b = level.astype(jnp.bfloat16)
    hidden_pre = jnp.dot(level_b, w_up, preferred_element_type=jnp.float32)
    hidden = exact_gelu(hidden_pre).astype(jnp.bfloat16)
    branch_out = jnp.dot(hidden, w_down, preferred_element_type=jnp.float32)
    branch_norm, branch_inv = layer_norm(branch_out)
    coarse = level + branch_norm
    upstream = cotangent.astype(jnp.float32).reshape(coarse.shape)
    slope_out = norm_slope(upstream, branch_norm, branch_inv).astype(jnp.bfloat16)
    slope_hidden = jnp.dot(slope_out, w_down.T, preferred_element_type=jnp.float32)
    _, pullback = jax.vjp(exact_gelu, hidden_pre)
    slope_pre = pullback(slope_hidden)[0].astype(jnp.bfloat16)
    grad_coarse = upstream + jnp.dot(slope_pre, w_up.T, preferred_element_type=jnp.float32)

    def banded(value):
        return value.reshape(N_ROWS, -1, value.shape[-1])

    def add_band(running, items):
        inputs_band, pre_band, hidden_band, out_band = items
        term_up = jnp.dot(inputs_band.T, pre_band, preferred_element_type=jnp.float32)
        term_down = jnp.dot(hidden_band.T, out_band, preferred_element_type=jnp.float32)
        term_up = lax.optimization_barrier(term_up.astype(jnp.bfloat16)).astype(jnp.float32)
        term_down = lax.optimization_barrier(term_down.astype(jnp.bfloat16)).astype(jnp.float32)
        return ((running[0] + term_up, running[1] + term_down), None)
    start_up = jnp.zeros((w_up.shape[0], w_up.shape[1]), jnp.float32)
    start_down = jnp.zeros((w_down.shape[0], w_down.shape[1]), jnp.float32)
    (grad_up, grad_down), _ = lax.scan(add_band, (start_up, start_down), (banded(level_b), banded(slope_pre), banded(hidden), banded(slope_out)))
    return (coarse.reshape(coarse_rows, coarse_cols, -1), grad_coarse.reshape(coarse_rows, coarse_cols, -1), grad_up, grad_down)
```

```python
import jax
import jax.numpy as jnp
from jax import lax
from jax.experimental import pallas as pl
from jax.experimental.pallas import tpu as pltpu
from jax.sharding import Mesh
from jax.sharding import PartitionSpec as P

WIN = 16
NX, NZ, NL, NCORE = 2, 8, 2, 2
ROWS = ("xh", "z")
COLS = ("xl", "core")
GRID = ("xh", "z", "xl", "core")
NROW, NCOL = NX * NZ, NL * NCORE

eps_norm = 1e-05
eps_unit = 1e-06
BF = jnp.bfloat16
F32 = jnp.float32


def dot(a, b):
    return jnp.dot(a, b, preferred_element_type=F32)


def dot_nt(a, b):
    return lax.dot_general(a, b, (((1,), (1,)), ((), ())), preferred_element_type=F32)


def dot_tn(a, b):
    return lax.dot_general(a, b, (((0,), (0,)), ((), ())), preferred_element_type=F32)


def layer_norm(value):
    average = jnp.mean(value, axis=-1, keepdims=True)
    centred = value - average
    spread = jnp.mean(centred * centred, axis=-1, keepdims=True)
    inverse = lax.rsqrt(spread + eps_norm)
    return (centred * inverse, inverse)


def norm_slope(upstream, normed, inverse):
    first_mean = jnp.mean(upstream, axis=-1, keepdims=True)
    second_mean = jnp.mean(upstream * normed, axis=-1, keepdims=True)
    return inverse * (upstream - first_mean - normed * second_mean)


def exact_gelu(value):
    return jax.nn.gelu(value, approximate=False)


def to_grid(array, dr, dc):
    pairs = [
        (r * NCOL + c, ((r + dr) % NROW) * NCOL + (c + dc) % NCOL)
        for r in range(NROW)
        for c in range(NCOL)
    ]
    return lax.ppermute(array, GRID, pairs)


def swap_cols(array, d):
    return lax.ppermute(array, COLS, [(i, i ^ d) for i in range(NCOL)])


def swap_half(array):
    return lax.ppermute(array, "xh", [(0, 1), (1, 0)])


def along_z(array, step):
    return lax.ppermute(array, "z", [(i, (i + step) % NZ) for i in range(NZ)])


def along_x(array, step, flip):
    pairs = []
    for x in range(4):
        for k in range(2):
            pairs.append((x * 2 + k, ((x + step) % 4) * 2 + (k ^ flip)))
    return lax.ppermute(array, ("xh", "xl", "core"), pairs)


def gather_rows(shard):
    other = swap_half(shard)
    first = lax.axis_index("xh") == 0
    own = jnp.stack([jnp.where(first, shard, other), jnp.where(first, other, shard)])
    z = lax.axis_index("z")
    full = jnp.zeros((NX, NZ, *shard.shape), shard.dtype)

    def put(full, block, k):
        return lax.dynamic_update_slice_in_dim(full, block[:, None], (z + k) % NZ, 1)

    full = put(full, own, 0)
    left = right = own
    for k in (1, 2, 3):
        left, right = along_z(left, -1), along_z(right, 1)
        full = put(full, left, k)
        full = put(full, right, NZ - k)
    far = jnp.stack([along_z(left[0], -1), along_z(right[1], 1)])
    full = put(full, far, 4)
    return full.reshape(NX * NZ * shard.shape[0], shard.shape[1])


def scatter_rows(term):
    blocks = term.reshape(NX, NZ, -1, term.shape[-1])
    z = lax.axis_index("z")

    def block(k):
        return lax.dynamic_index_in_dim(blocks, (z + k) % NZ, 1, False)

    far = block(4)
    left, right = along_z(far[0], -1), along_z(far[1], 1)
    near_left, near_right = block(NZ - 3), block(3)
    left = jnp.stack([near_left[0] + left, near_left[1]])
    right = jnp.stack([near_right[0], near_right[1] + right])
    for k in (2, 1):
        left, right = along_z(left, -1), along_z(right, 1)
        left, right = left + block(NZ - k), right + block(k)
    left, right = along_z(left, -1), along_z(right, 1)
    both = left.astype(F32) + right.astype(F32) + block(0).astype(F32)
    first = lax.axis_index("xh") == 0
    other = swap_half(jnp.where(first, both[1], both[0]).astype(term.dtype))
    return jnp.where(first, both[0], both[1]) + other.astype(F32)


def order_kernel(fields_ref, cot_ref, *outs):
    n = fields_ref.shape[0]
    to = lax.broadcasted_iota(jnp.int32, (n, n), 0)
    at = lax.broadcasted_iota(jnp.int32, (n, n), 1)
    c4, r4 = to & 3, (to >> 2) & 3
    pr, pc = (to >> 4) & 1, (to >> 5) & 1
    qb, qa = (to >> 6) & 1, (to >> 7) & 1
    source = (qa * 8 + r4 * 2 + pr) * 16 + qb * 8 + c4 * 2 + pc
    pick = jnp.where(at == source, 1.0, 0.0).astype(BF)
    moved = dot(pick, fields_ref[...].astype(BF)).astype(BF)
    m = cot_ref.shape[0]
    to = lax.broadcasted_iota(jnp.int32, (m, m), 0)
    at = lax.broadcasted_iota(jnp.int32, (m, m), 1)
    source = (((to >> 5) & 1) * 4 + ((to >> 2) & 3)) * 8 + ((to >> 4) & 1) * 4 + (to & 3)
    pick = jnp.where(at == source, 1.0, 0.0).astype(BF)
    cot = dot(pick, cot_ref[...]).astype(BF)
    for k in range(4):
        outs[k][...] = moved[k * 64 : (k + 1) * 64]
        outs[4 + k][...] = cot[k * 16 : (k + 1) * 16]


def window_kernel(scale_ref, x0, x1, x2, x3, qkv_ref, proj_ref, out_ref):
    quads = (x0[...], x1[...], x2[...], x3[...])
    x = jnp.concatenate([q[k * 16 : (k + 1) * 16] for k in range(4) for q in quads], axis=0)
    channels = x.shape[1]
    heads = channels // 64
    raw = dot(x, qkv_ref[...])
    mixed = []
    for h in range(heads):
        q = raw[:, h * 64 : (h + 1) * 64]
        k = raw[:, channels + h * 64 : channels + (h + 1) * 64]
        v = raw[:, 2 * channels + h * 64 : 2 * channels + (h + 1) * 64].astype(BF)
        q = q * lax.rsqrt(jnp.sum(q * q, axis=-1, keepdims=True) + eps_unit)
        k = k * lax.rsqrt(jnp.sum(k * k, axis=-1, keepdims=True) + eps_unit)
        scores = dot_nt(q.astype(BF), k.astype(BF))
        weights = jnp.exp(scores * scale_ref[h])
        total = jnp.sum(weights, axis=-1, keepdims=True)
        mixed.append(dot(weights.astype(BF), v) / total)
    mixed = jnp.concatenate(mixed, axis=1).astype(BF)
    normed, _ = layer_norm(dot(mixed, proj_ref[...]))
    out_ref[...] = (x.astype(F32) + normed).astype(BF)


def whole(count):
    return [pl.BlockSpec(memory_space=pltpu.VMEM)] * count


def local(fields, logit_scale, w_qkv, w_proj, w_merge, w_up, w_down, cotangent):
    tile_rows, tile_cols, channels = fields.shape
    wide = cotangent.shape[-1]
    tokens = tile_rows * tile_cols
    own = tokens // 4

    ordered = pl.pallas_call(
        order_kernel,
        out_shape=[jax.ShapeDtypeStruct((64, channels), BF)] * 4
        + [jax.ShapeDtypeStruct((16, wide), BF)] * 4,
        in_specs=whole(2),
        out_specs=whole(8),
        name="order",
    )(fields.reshape(tokens, channels), cotangent.reshape(own, wide))
    tile_quads, tile_cot = ordered[:4], ordered[4:]

    def to_window(quads):
        return (
            quads[3],
            to_grid(quads[2], 0, -1),
            to_grid(quads[1], -1, 0),
            to_grid(quads[0], -1, -1),
        )

    def to_tile(quads):
        return (
            to_grid(quads[3], 1, 1),
            to_grid(quads[2], 1, 0),
            to_grid(quads[1], 0, 1),
            quads[0],
        )

    x = to_window(tile_quads)

    half = w_merge.shape[0] // 2
    merge_parts = [w_merge, lax.ppermute(w_merge, "core", [(0, 1), (1, 0)])]
    merge_parts += [
        jnp.concatenate([along_x(w_merge[:half], 1, f), along_x(w_merge[half:], -1, f)], axis=0)
        for f in (0, 1)
    ]
    up_full = gather_rows(w_up)
    down_full = gather_rows(w_down.T)

    merged = pl.pallas_call(
        window_kernel,
        out_shape=jax.ShapeDtypeStruct((tokens, channels), BF),
        in_specs=[pl.BlockSpec(memory_space=pltpu.SMEM)] + whole(6),
        out_specs=pl.BlockSpec(memory_space=pltpu.VMEM),
        cost_estimate=pl.CostEstimate(
            flops=2 * tokens * channels * (4 * channels + 2 * tokens),
            transcendentals=tokens * tokens * 6,
            bytes_accessed=2_000_000,
        ),
        name="window",
    )(logit_scale, *x, w_qkv, w_proj)
    merged = jnp.concatenate([merged[k * own : (k + 1) * own] for k in range(4)], axis=1)

    parts = jnp.stack([dot(merged, w) for w in merge_parts]).reshape(2, 2, own, -1)
    parts = jnp.where(lax.axis_index("xl") == 0, parts, parts[::-1])
    parts = jnp.where(lax.axis_index("core") == 0, parts, parts[:, ::-1])
    level, _ = layer_norm(parts.transpose(2, 0, 1, 3).reshape(own, wide))
    level_own = level.astype(BF)
    level_b = jnp.concatenate([level_own] + [swap_cols(level_own, d) for d in (1, 2, 3)], axis=0)

    hidden_pre = dot(level_b, up_full)
    hidden = exact_gelu(hidden_pre).astype(BF)

    def to_owners(rows):
        rows = rows.astype(BF)
        total = rows[:own].astype(F32)
        for d in (1, 2, 3):
            total = total + swap_cols(rows[d * own : (d + 1) * own], d).astype(F32)
        return total

    branch_norm, branch_inv = layer_norm(to_owners(dot_nt(hidden, down_full)))
    coarse = level + branch_norm
    upstream = jnp.concatenate(to_window(tile_cot), axis=0).astype(F32)
    slope_own = norm_slope(upstream, branch_norm, branch_inv).astype(BF)
    slope_out = jnp.concatenate([slope_own] + [swap_cols(slope_own, d) for d in (1, 2, 3)], axis=0)
    slope_hidden = dot(slope_out, down_full)
    _, pullback = jax.vjp(exact_gelu, hidden_pre)
    slope_pre = pullback(slope_hidden)[0].astype(BF)
    grad_coarse = upstream + to_owners(dot_nt(slope_pre, up_full))
    term_down = dot_tn(slope_out, hidden).astype(BF)
    term_up = dot_tn(level_b, slope_pre).astype(BF)
    grad_down = scatter_rows(term_down).T
    grad_up = scatter_rows(term_up)

    def back(rows):
        rows = rows.astype(BF)
        quads = to_tile([rows[k * 16 : (k + 1) * 16] for k in range(4)])
        rows = jnp.stack(quads).reshape(2, 2, 4, 4, wide).transpose(0, 2, 1, 3, 4)
        return rows.reshape(tile_rows // 2, tile_cols // 2, wide).astype(F32)

    return (back(coarse), back(grad_coarse), grad_up, grad_down)


def solution(mesh):
    finer = Mesh(
        mesh.devices.reshape(NX, NZ, NL, NCORE, mesh.shape["dp"]),
        ("xh", "z", "xl", "core", "dp"),
    )
    rows = ("dp", *ROWS)
    in_specs = (
        P(rows, COLS, None),
        P(),
        P(),
        P(),
        P(None, COLS),
        P(ROWS, COLS),
        P(COLS, ROWS),
        P(rows, COLS, None),
    )
    out_specs = (
        P(rows, COLS, None),
        P(rows, COLS, None),
        P(ROWS, ("dp", *COLS)),
        P(COLS, rows),
    )
    return jax.shard_map(local, mesh=finer, in_specs=in_specs, out_specs=out_specs, check_vma=False)
```

```python
import jax
import jax.numpy as jnp
from jax import lax
from jax.experimental import pallas as pl
from jax.experimental.pallas import tpu as pltpu
from jax.sharding import Mesh
from jax.sharding import PartitionSpec as P

WIN = 16
NX, NZ, NL, NCORE = 2, 8, 2, 2
ROWS = ("xh", "z")
COLS = ("xl", "core")
GRID = ("xh", "z", "xl", "core")
NROW, NCOL = NX * NZ, NL * NCORE

eps_norm = 1e-05
eps_unit = 1e-06
BF = jnp.bfloat16
F32 = jnp.float32


def dot(a, b):
    return jnp.dot(a, b, preferred_element_type=F32)


def dot_nt(a, b):
    return lax.dot_general(a, b, (((1,), (1,)), ((), ())), preferred_element_type=F32)


def dot_tn(a, b):
    return lax.dot_general(a, b, (((0,), (0,)), ((), ())), preferred_element_type=F32)


def layer_norm(value):
    average = jnp.mean(value, axis=-1, keepdims=True)
    centred = value - average
    spread = jnp.mean(centred * centred, axis=-1, keepdims=True)
    inverse = lax.rsqrt(spread + eps_norm)
    return (centred * inverse, inverse)


def norm_slope(upstream, normed, inverse):
    first_mean = jnp.mean(upstream, axis=-1, keepdims=True)
    second_mean = jnp.mean(upstream * normed, axis=-1, keepdims=True)
    return inverse * (upstream - first_mean - normed * second_mean)


def exact_gelu(value):
    return jax.nn.gelu(value, approximate=False)


def to_grid(array, dr, dc):
    pairs = [
        (r * NCOL + c, ((r + dr) % NROW) * NCOL + (c + dc) % NCOL)
        for r in range(NROW)
        for c in range(NCOL)
    ]
    return lax.ppermute(array, GRID, pairs)


def swap_core(array):
    return lax.ppermute(array, "core", [(0, 1), (1, 0)])


def swap_xl(array):
    return lax.ppermute(array, "xl", [(0, 1), (1, 0)])


def swap_other(array):
    return lax.ppermute(array, ("xh", "xl"), [(0, 3), (3, 0), (1, 2), (2, 1)])


def swap_half(array):
    return lax.ppermute(array, "xh", [(0, 1), (1, 0)])


def along_z(array, step):
    return lax.ppermute(array, "z", [(i, (i + step) % NZ) for i in range(NZ)])


def gather_cols(rows):
    near = jnp.concatenate([rows, swap_xl(rows)], axis=0)
    return jnp.concatenate([near, swap_core(near)], axis=0)


def scatter_cols(rows):
    rows = rows.astype(BF)
    half, quarter = rows.shape[0] // 2, rows.shape[0] // 4
    near = rows[:half].astype(F32) + swap_core(rows[half:]).astype(F32)
    return near[:quarter] + swap_xl(near[quarter:].astype(BF)).astype(F32)


def gather_rows(shard):
    other = swap_half(shard)
    first = lax.axis_index("xh") == 0
    own = jnp.stack([jnp.where(first, shard, other), jnp.where(first, other, shard)])
    z = lax.axis_index("z")
    full = jnp.zeros((NX, NZ, *shard.shape), shard.dtype)

    def put(full, block, k):
        return lax.dynamic_update_slice_in_dim(full, block[:, None], (z + k) % NZ, 1)

    full = put(full, own, 0)
    left = right = own
    for k in (1, 2, 3):
        left, right = along_z(left, -1), along_z(right, 1)
        full = put(full, left, k)
        full = put(full, right, NZ - k)
    far = jnp.stack([along_z(left[0], -1), along_z(right[1], 1)])
    return put(full, far, 4)


def scatter_rows(terms):
    blocks = [term.reshape(NX, NZ, -1, term.shape[-1]) for term in terms]
    z = lax.axis_index("z")

    def block(k):
        return jnp.stack([lax.dynamic_index_in_dim(b, (z + k) % NZ, 1, False) for b in blocks], 1)

    far = block(4)
    left, right = along_z(far[0], -1), along_z(far[1], 1)
    near_left, near_right = block(NZ - 3), block(3)
    left = jnp.stack([near_left[0] + left, near_left[1]])
    right = jnp.stack([near_right[0], near_right[1] + right])
    for k in (2, 1):
        left, right = along_z(left, -1), along_z(right, 1)
        left, right = left + block(NZ - k), right + block(k)
    left, right = along_z(left, -1), along_z(right, 1)
    both = left.astype(F32) + right.astype(F32) + block(0).astype(F32)
    first = lax.axis_index("xh") == 0
    other = swap_half(jnp.where(first, both[1], both[0]).astype(BF))
    return jnp.where(first, both[0], both[1]) + other.astype(F32)


def order_kernel(fields_ref, cot_ref, *outs):
    n = fields_ref.shape[0]
    to = lax.broadcasted_iota(jnp.int32, (n, n), 0)
    at = lax.broadcasted_iota(jnp.int32, (n, n), 1)
    c4, r4 = to & 3, (to >> 2) & 3
    pr, pc = (to >> 4) & 1, (to >> 5) & 1
    qb, qa = (to >> 6) & 1, (to >> 7) & 1
    source = (qa * 8 + r4 * 2 + pr) * 16 + qb * 8 + c4 * 2 + pc
    pick = jnp.where(at == source, 1.0, 0.0).astype(BF)
    moved = dot(pick, fields_ref[...].astype(BF)).astype(BF)
    m = cot_ref.shape[0]
    to = lax.broadcasted_iota(jnp.int32, (m, m), 0)
    at = lax.broadcasted_iota(jnp.int32, (m, m), 1)
    source = (((to >> 5) & 1) * 4 + ((to >> 2) & 3)) * 8 + ((to >> 4) & 1) * 4 + (to & 3)
    pick = jnp.where(at == source, 1.0, 0.0).astype(BF)
    cot = dot(pick, cot_ref[...]).astype(BF)
    wide = fields_ref.shape[1]
    for k in range(4):
        outs[k][:64] = moved[k * 64 : (k + 1) * 64]
        outs[k][64:80] = cot[k * 16 : (k + 1) * 16, :wide]
        outs[k][80:] = cot[k * 16 : (k + 1) * 16, wide:]


def window_kernel(scale_ref, x0, x1, x2, x3, qkv_ref, proj_ref, out_ref):
    quads = (x0[...], x1[...], x2[...], x3[...])
    x = jnp.concatenate([q[k * 16 : (k + 1) * 16] for k in range(4) for q in quads], axis=0)
    channels = x.shape[1]
    heads = channels // 64
    raw = dot(x, qkv_ref[...])
    mixed = []
    for h in range(heads):
        q = raw[:, h * 64 : (h + 1) * 64]
        k = raw[:, channels + h * 64 : channels + (h + 1) * 64]
        v = raw[:, 2 * channels + h * 64 : 2 * channels + (h + 1) * 64].astype(BF)
        q = q * lax.rsqrt(jnp.sum(q * q, axis=-1, keepdims=True) + eps_unit)
        k = k * lax.rsqrt(jnp.sum(k * k, axis=-1, keepdims=True) + eps_unit)
        scores = dot_nt(q.astype(BF), k.astype(BF))
        weights = jnp.exp(scores * scale_ref[h])
        total = jnp.sum(weights, axis=-1, keepdims=True)
        mixed.append(dot(weights.astype(BF), v) / total)
    mixed = jnp.concatenate(mixed, axis=1).astype(BF)
    normed, _ = layer_norm(dot(mixed, proj_ref[...]))
    out_ref[...] = (x.astype(F32) + normed).astype(BF)


def whole(count):
    return [pl.BlockSpec(memory_space=pltpu.VMEM)] * count


def local(fields, logit_scale, w_qkv, w_proj, w_merge, w_up, w_down, cotangent):
    tile_rows, tile_cols, channels = fields.shape
    wide = cotangent.shape[-1]
    tokens = tile_rows * tile_cols
    own = tokens // 4

    tile_quads = pl.pallas_call(
        order_kernel,
        out_shape=[jax.ShapeDtypeStruct((96, channels), BF)] * 4,
        in_specs=whole(2),
        out_specs=whole(4),
        name="order",
    )(fields.reshape(tokens, channels), cotangent.reshape(own, wide))

    def to_window(quads):
        return (
            quads[3],
            to_grid(quads[2], 0, -1),
            to_grid(quads[1], -1, 0),
            to_grid(quads[0], -1, -1),
        )

    def to_tile(quads):
        return (
            to_grid(quads[3], 1, 1),
            to_grid(quads[2], 1, 0),
            to_grid(quads[1], 0, 1),
            quads[0],
        )

    x = to_window(tile_quads)

    weights = gather_rows(jnp.stack([w_up, w_down.T]))
    up_full = weights[:, :, 0].reshape(wide, -1)
    down_full = weights[:, :, 1].reshape(wide, -1)

    merge_own = w_merge.T
    half = merge_own.shape[0] // 2
    merge_far = jnp.concatenate([swap_xl(merge_own[:half]), swap_other(merge_own[half:])], axis=0)
    merge_parts = [merge_own, swap_core(merge_own), merge_far, swap_core(merge_far)]

    merged = pl.pallas_call(
        window_kernel,
        out_shape=jax.ShapeDtypeStruct((tokens, channels), BF),
        in_specs=[pl.BlockSpec(memory_space=pltpu.SMEM)] + whole(6),
        out_specs=pl.BlockSpec(memory_space=pltpu.VMEM),
        cost_estimate=pl.CostEstimate(
            flops=2 * tokens * channels * (4 * channels + 2 * tokens),
            transcendentals=tokens * tokens * 6,
            bytes_accessed=2_000_000,
        ),
        name="window",
    )(logit_scale, *x, w_qkv, w_proj)
    merged = jnp.concatenate([merged[k * own : (k + 1) * own] for k in range(4)], axis=1)

    parts = jnp.stack([dot_nt(merged, w) for w in merge_parts]).reshape(2, 2, own, -1)
    parts = jnp.where(lax.axis_index("xl") == 0, parts, parts[::-1])
    parts = jnp.where(lax.axis_index("core") == 0, parts, parts[:, ::-1])
    level, _ = layer_norm(parts.transpose(2, 0, 1, 3).reshape(own, wide))
    level_b = gather_cols(level.astype(BF))

    hidden_pre = dot(level_b, up_full)
    hidden = exact_gelu(hidden_pre).astype(BF)

    branch_norm, branch_inv = layer_norm(scatter_cols(dot_nt(hidden, down_full)))
    coarse = level + branch_norm
    upstream = jnp.concatenate(
        [jnp.concatenate([q[64:80], q[80:96]], axis=1) for q in x], axis=0
    ).astype(F32)
    slope_own = norm_slope(upstream, branch_norm, branch_inv).astype(BF)
    slope_out = gather_cols(slope_own)
    slope_hidden = dot(slope_out, down_full)
    _, pullback = jax.vjp(exact_gelu, hidden_pre)
    slope_pre = pullback(slope_hidden)[0].astype(BF)
    term_down = dot_tn(slope_out, hidden).astype(BF)
    term_up = dot_tn(level_b, slope_pre).astype(BF)
    grads = scatter_rows((term_down, term_up))
    grad_coarse = upstream + scatter_cols(dot_nt(slope_pre, up_full))

    both = jnp.concatenate([coarse, grad_coarse], axis=1).astype(BF)
    quads = to_tile([both[k * 16 : (k + 1) * 16] for k in range(4)])
    both = jnp.stack(quads).reshape(2, 2, 4, 4, 2 * wide).transpose(0, 2, 1, 3, 4)
    both = both.reshape(tile_rows // 2, tile_cols // 2, 2 * wide).astype(F32)
    return (both[..., :wide], both[..., wide:], grads[1], grads[0].T)


def solution(mesh):
    finer = Mesh(
        mesh.devices.reshape(NX, NZ, NL, NCORE, mesh.shape["dp"]),
        ("xh", "z", "xl", "core", "dp"),
    )
    rows = ("dp", *ROWS)
    in_specs = (
        P(rows, COLS, None),
        P(),
        P(),
        P(),
        P(None, COLS),
        P(ROWS, COLS),
        P(COLS, ROWS),
        P(rows, COLS, None),
    )
    out_specs = (
        P(rows, COLS, None),
        P(rows, COLS, None),
        P(ROWS, ("dp", *COLS)),
        P(COLS, rows),
    )
    return jax.shard_map(local, mesh=finer, in_specs=in_specs, out_specs=out_specs, check_vma=False)
```

```python
import jax
import jax.numpy as jnp
from jax import lax
from jax.experimental import pallas as pl
from jax.experimental.pallas import tpu as pltpu
from jax.sharding import Mesh
from jax.sharding import PartitionSpec as P


NX, NZ, NL, NCORE = 2, 8, 2, 2
ROWS = ("xh", "z")
COLS = ("xl", "core")
GRID = ("xh", "z", "xl", "core")
NROW, NCOL = NX * NZ, NL * NCORE

eps_norm = 1e-05
eps_unit = 1e-06
BF = jnp.bfloat16
F32 = jnp.float32


def dot(a, b):
    return jnp.dot(a, b, preferred_element_type=F32)


def dot_nt(a, b):
    return lax.dot_general(a, b, (((1,), (1,)), ((), ())), preferred_element_type=F32)


def dot_tn(a, b):
    return lax.dot_general(a, b, (((0,), (0,)), ((), ())), preferred_element_type=F32)


def layer_norm(value):
    average = jnp.mean(value, axis=-1, keepdims=True)
    centred = value - average
    spread = jnp.mean(centred * centred, axis=-1, keepdims=True)
    inverse = lax.rsqrt(spread + eps_norm)
    return (centred * inverse, inverse)


def norm_slope(upstream, normed, inverse):
    first_mean = jnp.mean(upstream, axis=-1, keepdims=True)
    second_mean = jnp.mean(upstream * normed, axis=-1, keepdims=True)
    return inverse * (upstream - first_mean - normed * second_mean)


def exact_gelu(value):
    return jax.nn.gelu(value, approximate=False)


def to_grid(array, dr, dc):
    pairs = [
        (r * NCOL + c, ((r + dr) % NROW) * NCOL + (c + dc) % NCOL)
        for r in range(NROW)
        for c in range(NCOL)
    ]
    return lax.ppermute(array, GRID, pairs)


def swap_core(array):
    return lax.ppermute(array, "core", [(0, 1), (1, 0)])


def swap_xl(array):
    return lax.ppermute(array, "xl", [(0, 1), (1, 0)])


def swap_half(array):
    return lax.ppermute(array, "xh", [(0, 1), (1, 0)])


def along_z(array, step):
    return lax.ppermute(array, "z", [(i, (i + step) % NZ) for i in range(NZ)])


def gather_cols(rows):
    near = jnp.concatenate([rows, swap_xl(rows)], axis=0)
    return jnp.concatenate([near, swap_core(near)], axis=0)


def scatter_cols(rows):
    rows = rows.astype(BF)
    half, quarter = rows.shape[0] // 2, rows.shape[0] // 4
    near = rows[:half].astype(F32) + swap_core(rows[half:]).astype(F32)
    return near[:quarter] + swap_xl(near[quarter:].astype(BF)).astype(F32)


def gather_rows(shard):
    other = swap_half(shard)
    first = lax.axis_index("xh") == 0
    own = jnp.stack([jnp.where(first, shard, other), jnp.where(first, other, shard)])
    z = lax.axis_index("z")
    full = jnp.zeros((NX, NZ, *shard.shape), shard.dtype)

    def put(full, block, k):
        return lax.dynamic_update_slice_in_dim(full, block[:, None], (z + k) % NZ, 1)

    full = put(full, own, 0)
    left = right = own
    for k in (1, 2, 3):
        left, right = along_z(left, -1), along_z(right, 1)
        full = put(full, left, k)
        full = put(full, right, NZ - k)
    far = [along_z(left[0], -1), along_z(right[1], 1)]
    far = jnp.stack(far)
    return put(full, far, 4)


def scatter_rows(terms):
    blocks = [term.reshape(NX, NZ, -1, term.shape[-1]) for term in terms]
    z = lax.axis_index("z")

    def block(k):
        return jnp.stack([lax.dynamic_index_in_dim(b, (z + k) % NZ, 1, False) for b in blocks], 1)

    far = block(4)
    left, right = along_z(far[0], -1), along_z(far[1], 1)
    near_left, near_right = block(NZ - 3), block(3)
    left = jnp.stack([near_left[0] + left, near_left[1]])
    right = jnp.stack([near_right[0], near_right[1] + right])
    for k in (2, 1):
        left, right = along_z(left, -1), along_z(right, 1)
        left, right = left + block(NZ - k), right + block(k)
    left, right = along_z(left, -1), along_z(right, 1)
    both = left.astype(F32) + right.astype(F32) + block(0).astype(F32)
    first = lax.axis_index("xh") == 0
    other = swap_half(jnp.where(first, both[1], both[0]).astype(BF))
    return jnp.where(first, both[0], both[1]) + other.astype(F32)


def order_kernel(fields_ref, cot_ref, *outs):
    n = fields_ref.shape[0]
    to = lax.broadcasted_iota(jnp.int32, (n, n), 0)
    at = lax.broadcasted_iota(jnp.int32, (n, n), 1)
    c4, r4 = to & 3, (to >> 2) & 3
    pr, pc = (to >> 4) & 1, (to >> 5) & 1
    qb, qa = (to >> 6) & 1, (to >> 7) & 1
    source = (qa * 8 + r4 * 2 + pr) * 16 + qb * 8 + c4 * 2 + pc
    pick = jnp.where(at == source, 1.0, 0.0).astype(BF)
    moved = dot(pick, fields_ref[...].astype(BF)).astype(BF)
    m = cot_ref.shape[0]
    to = lax.broadcasted_iota(jnp.int32, (m, m), 0)
    at = lax.broadcasted_iota(jnp.int32, (m, m), 1)
    source = (((to >> 5) & 1) * 4 + ((to >> 2) & 3)) * 8 + ((to >> 4) & 1) * 4 + (to & 3)
    pick = jnp.where(at == source, 1.0, 0.0).astype(BF)
    cot = dot(pick, cot_ref[...]).astype(BF)
    wide = fields_ref.shape[1]
    for k in range(4):
        outs[k][:64] = moved[k * 64 : (k + 1) * 64]
        outs[k][64:80] = cot[k * 16 : (k + 1) * 16, :wide]
        outs[k][80:] = cot[k * 16 : (k + 1) * 16, wide:]


def window_kernel(scale_ref, x0, x1, x2, x3, qkv_ref, proj_ref, out_ref, cot_ref):
    quads = (x0[...], x1[...], x2[...], x3[...])
    x = jnp.concatenate([q[k * 16 : (k + 1) * 16] for k in range(4) for q in quads], axis=0)
    channels = x.shape[1]
    heads = channels // 64
    raw = dot(x, qkv_ref[...])
    mixed = []
    for h in range(heads):
        q = raw[:, h * 64 : (h + 1) * 64]
        k = raw[:, channels + h * 64 : channels + (h + 1) * 64]
        v = raw[:, 2 * channels + h * 64 : 2 * channels + (h + 1) * 64].astype(BF)
        q = q * lax.rsqrt(jnp.sum(q * q, axis=-1, keepdims=True) + eps_unit)
        k = k * lax.rsqrt(jnp.sum(k * k, axis=-1, keepdims=True) + eps_unit)
        scores = dot_nt(q.astype(BF), k.astype(BF))
        weights = jnp.exp(scores * scale_ref[h])
        total = jnp.sum(weights, axis=-1, keepdims=True)
        mixed.append(dot(weights.astype(BF), v) / total)
    mixed = jnp.concatenate(mixed, axis=1).astype(BF)
    normed, _ = layer_norm(dot(mixed, proj_ref[...]))
    stream = (x.astype(F32) + normed).astype(BF)
    own = stream.shape[0] // 4
    for k in range(4):
        out_ref[:, k * channels : (k + 1) * channels] = stream[k * own : (k + 1) * own]
        cot_ref[k * 16 : (k + 1) * 16, :channels] = quads[k][64:80]
        cot_ref[k * 16 : (k + 1) * 16, channels:] = quads[k][80:]


def level_kernel(merged_ref, own_ref, core_ref, near_ref, far_ref, place_ref, level_ref, bf_ref):
    merged = merged_ref[...]
    parts = [dot_nt(merged, r[...]) for r in (own_ref, core_ref, near_ref, far_ref)]
    xl, core = place_ref[0] == 0, place_ref[1] == 0
    low = [jnp.where(xl, parts[k], parts[k + 2]) for k in (0, 1)]
    high = [jnp.where(xl, parts[k + 2], parts[k]) for k in (0, 1)]
    ordered = []
    for pair in (low, high):
        ordered += [jnp.where(core, pair[0], pair[1]), jnp.where(core, pair[1], pair[0])]
    level, _ = layer_norm(jnp.concatenate(ordered, axis=1))
    level_ref[...] = level
    bf_ref[...] = level.astype(BF)


def whole(count):
    return [pl.BlockSpec(memory_space=pltpu.VMEM)] * count


def whole_step(fields, logit_scale, w_qkv, w_proj, w_merge, w_up, w_down, cotangent):
    tile_rows, tile_cols, channels = fields.shape
    wide = cotangent.shape[-1]
    tokens = tile_rows * tile_cols
    own = tokens // 4

    tile_quads = pl.pallas_call(
        order_kernel,
        out_shape=[jax.ShapeDtypeStruct((96, channels), BF)] * 4,
        in_specs=whole(2),
        out_specs=whole(4),
        name="order",
    )(fields.reshape(tokens, channels), cotangent.reshape(own, wide))

    def to_window(quads):
        return (
            quads[3],
            to_grid(quads[2], 0, -1),
            to_grid(quads[1], -1, 0),
            to_grid(quads[0], -1, -1),
        )

    def to_tile(quads):
        return (
            to_grid(quads[3], 1, 1),
            to_grid(quads[2], 1, 0),
            to_grid(quads[1], 0, 1),
            quads[0],
        )

    x = to_window(tile_quads)

    weights = gather_rows(jnp.stack([w_up, w_down.T]))
    up_full = weights[:, :, 0].reshape(wide, -1)
    down_full = weights[:, :, 1].reshape(wide, -1)

    merge_own = w_merge.T
    merge_near = swap_xl(merge_own)
    merge_core = swap_core(merge_own)
    merge_far = swap_core(merge_near)

    merged, cot = pl.pallas_call(
        window_kernel,
        out_shape=[
            jax.ShapeDtypeStruct((own, 4 * channels), BF),
            jax.ShapeDtypeStruct((own, wide), BF),
        ],
        in_specs=[pl.BlockSpec(memory_space=pltpu.SMEM)] + whole(6),
        out_specs=whole(2),
        cost_estimate=pl.CostEstimate(
            flops=2 * tokens * channels * (4 * channels + 2 * tokens),
            transcendentals=tokens * tokens * 6,
            bytes_accessed=2_000_000,
        ),
        name="window",
    )(logit_scale, *x, w_qkv, w_proj)
    place = jnp.stack([lax.axis_index("xl"), lax.axis_index("core")])
    level, level_own = pl.pallas_call(
        level_kernel,
        out_shape=[jax.ShapeDtypeStruct((own, wide), F32), jax.ShapeDtypeStruct((own, wide), BF)],
        in_specs=whole(5) + [pl.BlockSpec(memory_space=pltpu.SMEM)],
        out_specs=whole(2),
        cost_estimate=pl.CostEstimate(
            flops=8 * own * channels * wide, transcendentals=own, bytes_accessed=3_000_000
        ),
        name="level",
    )(merged, merge_own, merge_core, merge_near, merge_far, place)
    level_b = gather_cols(level_own)

    hidden_pre = dot(level_b, up_full)
    hidden = exact_gelu(hidden_pre).astype(BF)

    branch_norm, branch_inv = layer_norm(scatter_cols(dot_nt(hidden, down_full)))
    coarse = level + branch_norm
    upstream = cot.astype(F32)
    slope_own = norm_slope(upstream, branch_norm, branch_inv).astype(BF)
    slope_out = gather_cols(slope_own)
    slope_hidden = dot(slope_out, down_full)
    _, pullback = jax.vjp(exact_gelu, hidden_pre)
    slope_pre = pullback(slope_hidden)[0].astype(BF)
    term_down = dot_tn(slope_out, hidden).astype(BF)
    term_up = dot_tn(level_b, slope_pre).astype(BF)
    grads = scatter_rows((term_down, term_up))
    grad_coarse = upstream + scatter_cols(dot_nt(slope_pre, up_full))

    both = jnp.concatenate([coarse, grad_coarse], axis=1).astype(BF)
    quads = to_tile([both[k * 16 : (k + 1) * 16] for k in range(4)])
    both = jnp.stack(quads).reshape(2, 2, 4, 4, 2 * wide).transpose(0, 2, 1, 3, 4)
    both = both.reshape(tile_rows // 2, tile_cols // 2, 2 * wide).astype(F32)
    return (both[..., :wide], both[..., wide:], grads[1], grads[0].T)


def solution(mesh):
    finer = Mesh(
        mesh.devices.reshape(NX, NZ, NL, NCORE, mesh.shape["dp"]),
        ("xh", "z", "xl", "core", "dp"),
    )
    rows = ("dp", *ROWS)
    in_specs = (
        P(rows, COLS, None),
        P(),
        P(),
        P(),
        P(None, COLS),
        P(ROWS, COLS),
        P(COLS, ROWS),
        P(rows, COLS, None),
    )
    out_specs = (
        P(rows, COLS, None),
        P(rows, COLS, None),
        P(ROWS, ("dp", *COLS)),
        P(COLS, rows),
    )
    return jax.shard_map(
        whole_step, mesh=finer, in_specs=in_specs, out_specs=out_specs, check_vma=False
    )
```

```python
import jax
import jax.numpy as jnp
from jax import lax
from jax.experimental import pallas as pl
from jax.experimental.pallas import tpu as pltpu
from jax.sharding import Mesh
from jax.sharding import PartitionSpec as P


NX, NZ, NL, NCORE = 2, 8, 2, 2
ROWS = ("xh", "z")
COLS = ("xl", "core")
GRID = ("xh", "z", "xl", "core")
NROW, NCOL = NX * NZ, NL * NCORE

eps_norm = 1e-05
eps_unit = 1e-06
BF = jnp.bfloat16
F32 = jnp.float32


def dot(a, b):
    return jnp.dot(a, b, preferred_element_type=F32)


def dot_nt(a, b):
    return lax.dot_general(a, b, (((1,), (1,)), ((), ())), preferred_element_type=F32)


def dot_tn(a, b):
    return lax.dot_general(a, b, (((0,), (0,)), ((), ())), preferred_element_type=F32)


def layer_norm(value):
    average = jnp.mean(value, axis=-1, keepdims=True)
    centred = value - average
    spread = jnp.mean(centred * centred, axis=-1, keepdims=True)
    inverse = lax.rsqrt(spread + eps_norm)
    return (centred * inverse, inverse)


def norm_slope(upstream, normed, inverse):
    first_mean = jnp.mean(upstream, axis=-1, keepdims=True)
    second_mean = jnp.mean(upstream * normed, axis=-1, keepdims=True)
    return inverse * (upstream - first_mean - normed * second_mean)


def exact_gelu(value):
    return jax.nn.gelu(value, approximate=False)


def to_grid(array, dr, dc):
    pairs = [
        (r * NCOL + c, ((r + dr) % NROW) * NCOL + (c + dc) % NCOL)
        for r in range(NROW)
        for c in range(NCOL)
    ]
    return lax.ppermute(array, GRID, pairs)


def swap_core(array):
    return lax.ppermute(array, "core", [(0, 1), (1, 0)])


def swap_xl(array):
    return lax.ppermute(array, "xl", [(0, 1), (1, 0)])


def swap_half(array):
    return lax.ppermute(array, "xh", [(0, 1), (1, 0)])


def along_z(array, step):
    return lax.ppermute(array, "z", [(i, (i + step) % NZ) for i in range(NZ)])


def across_z(array, step):
    pairs = []
    for h in range(NX):
        for i in range(NZ):
            pairs.append((h * NZ + i, (1 - h) * NZ + (i + step) % NZ))
    return lax.ppermute(array, ROWS, pairs)


def gather_cols(rows):
    other = swap_xl(rows)
    near = jnp.concatenate([rows, other], axis=0)
    across = swap_core(near)
    return jnp.concatenate([near, across], axis=0)


def scatter_cols(rows):
    rows = rows.astype(BF)
    half, quarter = rows.shape[0] // 2, rows.shape[0] // 4
    near = rows[:half].astype(F32) + swap_core(rows[half:]).astype(F32)
    return near[:quarter] + swap_xl(near[quarter:].astype(BF)).astype(F32)


def gather_rows(shard):
    other = swap_half(shard)
    first = lax.axis_index("xh") == 0
    own = jnp.stack([jnp.where(first, shard, other), jnp.where(first, other, shard)])
    z = lax.axis_index("z")
    full = jnp.zeros((NX, NZ, *shard.shape), shard.dtype)

    def put(full, block, k):
        return lax.dynamic_update_slice_in_dim(full, block[:, None], (z + k) % NZ, 1)

    full = put(full, own, 0)
    left = right = own
    for k in (1, 2, 3):
        left, right = along_z(left, -1), along_z(right, 1)
        full = put(full, left, k)
        full = put(full, right, NZ - k)
    far = [along_z(left[0], -1), along_z(right[1], 1)]
    far = jnp.stack(far)
    return put(full, far, 4)


def scatter_rows(terms):
    blocks = [term.reshape(NX, NZ, -1, term.shape[-1]) for term in terms]
    z = lax.axis_index("z")

    def block(k):
        return jnp.stack([lax.dynamic_index_in_dim(b, (z + k) % NZ, 1, False) for b in blocks], 1)

    own = block(0)
    own_other = swap_half(jnp.where(lax.axis_index("xh") == 0, own[1], own[0]))
    far = block(4)
    left, right = along_z(far[0], -1), along_z(far[1], 1)
    near_left, near_right = block(NZ - 3), block(3)
    left = jnp.stack([near_left[0] + left, near_left[1]])
    right = jnp.stack([near_right[0], near_right[1] + right])
    for k in (2, 1):
        left, right = along_z(left, -1), along_z(right, 1)
        left, right = left + block(NZ - k), right + block(k)
    first = lax.axis_index("xh") == 0

    def mine(v):
        return jnp.where(first, v[0], v[1])

    def theirs(v):
        return jnp.where(first, v[1], v[0])

    near = [along_z(mine(left), -1), along_z(mine(right), 1)]
    cross = [across_z(theirs(left), -1), across_z(theirs(right), 1)]
    total = mine(own).astype(F32) + own_other.astype(F32)
    for part in near + cross:
        total = total + part.astype(F32)
    return total


def order_kernel(fields_ref, cot_ref, *outs):
    n = fields_ref.shape[0]
    to = lax.broadcasted_iota(jnp.int32, (n, n), 0)
    at = lax.broadcasted_iota(jnp.int32, (n, n), 1)
    c4, r4 = to & 3, (to >> 2) & 3
    pr, pc = (to >> 4) & 1, (to >> 5) & 1
    qb, qa = (to >> 6) & 1, (to >> 7) & 1
    source = (qa * 8 + r4 * 2 + pr) * 16 + qb * 8 + c4 * 2 + pc
    pick = jnp.where(at == source, 1.0, 0.0).astype(BF)
    moved = dot(pick, fields_ref[...].astype(BF)).astype(BF)
    m = cot_ref.shape[0]
    to = lax.broadcasted_iota(jnp.int32, (m, m), 0)
    at = lax.broadcasted_iota(jnp.int32, (m, m), 1)
    source = (((to >> 5) & 1) * 4 + ((to >> 2) & 3)) * 8 + ((to >> 4) & 1) * 4 + (to & 3)
    pick = jnp.where(at == source, 1.0, 0.0).astype(BF)
    cot = dot(pick, cot_ref[...]).astype(BF)
    wide = fields_ref.shape[1]
    for k in range(4):
        outs[k][:64] = moved[k * 64 : (k + 1) * 64]
        outs[k][64:80] = cot[k * 16 : (k + 1) * 16, :wide]
        outs[k][80:] = cot[k * 16 : (k + 1) * 16, wide:]


def window_kernel(scale_ref, x0, x1, x2, x3, qkv_ref, proj_ref, out_ref, cot_ref):
    quads = (x0[...], x1[...], x2[...], x3[...])
    x = jnp.concatenate([q[k * 16 : (k + 1) * 16] for k in range(4) for q in quads], axis=0)
    channels = x.shape[1]
    heads = channels // 64
    raw = dot(x, qkv_ref[...])
    mixed = []
    for h in range(heads):
        q = raw[:, h * 64 : (h + 1) * 64]
        k = raw[:, channels + h * 64 : channels + (h + 1) * 64]
        v = raw[:, 2 * channels + h * 64 : 2 * channels + (h + 1) * 64].astype(BF)
        q = q * lax.rsqrt(jnp.sum(q * q, axis=-1, keepdims=True) + eps_unit)
        k = k * lax.rsqrt(jnp.sum(k * k, axis=-1, keepdims=True) + eps_unit)
        scores = dot_nt(q.astype(BF), k.astype(BF))
        weights = jnp.exp(scores * scale_ref[h])
        total = jnp.sum(weights, axis=-1, keepdims=True)
        mixed.append(dot(weights.astype(BF), v) / total)
    mixed = jnp.concatenate(mixed, axis=1).astype(BF)
    normed, _ = layer_norm(dot(mixed, proj_ref[...]))
    stream = (x.astype(F32) + normed).astype(BF)
    own = stream.shape[0] // 4
    for k in range(4):
        out_ref[:, k * channels : (k + 1) * channels] = stream[k * own : (k + 1) * own]
        cot_ref[k * 16 : (k + 1) * 16, :channels] = quads[k][64:80]
        cot_ref[k * 16 : (k + 1) * 16, channels:] = quads[k][80:]


def level_kernel(merged_ref, own_ref, core_ref, near_ref, far_ref, level_ref, bf_ref):
    merged = merged_ref[...]
    parts = [dot_nt(merged, r[...]) for r in (own_ref, core_ref, near_ref, far_ref)]
    xl, core = lax.axis_index("xl") == 0, lax.axis_index("core") == 0
    low = [jnp.where(xl, parts[k], parts[k + 2]) for k in (0, 1)]
    high = [jnp.where(xl, parts[k + 2], parts[k]) for k in (0, 1)]
    ordered = []
    for pair in (low, high):
        ordered += [jnp.where(core, pair[0], pair[1]), jnp.where(core, pair[1], pair[0])]
    level, _ = layer_norm(jnp.concatenate(ordered, axis=1))
    level_ref[...] = level
    bf_ref[...] = level.astype(BF)


def whole(count):
    return [pl.BlockSpec(memory_space=pltpu.VMEM)] * count


def whole_step(fields, logit_scale, w_qkv, w_proj, w_merge, w_up, w_down, cotangent):
    tile_rows, tile_cols, channels = fields.shape
    wide = cotangent.shape[-1]
    tokens = tile_rows * tile_cols
    own = tokens // 4

    tile_quads = pl.pallas_call(
        order_kernel,
        out_shape=[jax.ShapeDtypeStruct((96, channels), BF)] * 4,
        in_specs=whole(2),
        out_specs=whole(4),
        name="order",
    )(fields.reshape(tokens, channels), cotangent.reshape(own, wide))

    def to_window(quads):
        return (
            quads[3],
            to_grid(quads[2], 0, -1),
            to_grid(quads[1], -1, 0),
            to_grid(quads[0], -1, -1),
        )

    def to_tile(quads):
        return (
            to_grid(quads[3], 1, 1),
            to_grid(quads[2], 1, 0),
            to_grid(quads[1], 0, 1),
            quads[0],
        )

    x = to_window(tile_quads)

    weights = gather_rows(jnp.stack([w_up, w_down.T]))
    up_full = weights[:, :, 0].reshape(wide, -1)
    down_full = weights[:, :, 1].reshape(wide, -1)

    merge_own = w_merge.T
    merge_near = swap_xl(merge_own)
    merge_core = swap_core(merge_own)
    merge_far = swap_core(merge_near)

    merged, cot = pl.pallas_call(
        window_kernel,
        out_shape=[
            jax.ShapeDtypeStruct((own, 4 * channels), BF),
            jax.ShapeDtypeStruct((own, wide), BF),
        ],
        in_specs=[pl.BlockSpec(memory_space=pltpu.SMEM)] + whole(6),
        out_specs=whole(2),
        cost_estimate=pl.CostEstimate(
            flops=2 * tokens * channels * (4 * channels + 2 * tokens),
            transcendentals=tokens * tokens * 6,
            bytes_accessed=2_000_000,
        ),
        name="window",
    )(
        logit_scale,
        *x,
        pltpu.with_memory_space_constraint(w_qkv, pltpu.VMEM),
        pltpu.with_memory_space_constraint(w_proj, pltpu.VMEM),
    )
    level, level_own = pl.pallas_call(
        level_kernel,
        out_shape=[jax.ShapeDtypeStruct((own, wide), F32), jax.ShapeDtypeStruct((own, wide), BF)],
        in_specs=whole(5),
        out_specs=whole(2),
        cost_estimate=pl.CostEstimate(
            flops=8 * own * channels * wide, transcendentals=own, bytes_accessed=3_000_000
        ),
        name="level",
    )(merged, merge_own, merge_core, merge_near, merge_far)
    level_b = gather_cols(level_own)

    hidden_pre = dot(level_b, up_full)
    hidden = exact_gelu(hidden_pre).astype(BF)

    branch_norm, branch_inv = layer_norm(scatter_cols(dot_nt(hidden, down_full)))
    coarse = level + branch_norm
    upstream = cot.astype(F32)
    slope_own = norm_slope(upstream, branch_norm, branch_inv).astype(BF)
    slope_out = gather_cols(slope_own)
    slope_hidden = dot(slope_out, down_full)
    _, pullback = jax.vjp(exact_gelu, hidden_pre)
    slope_pre = pullback(slope_hidden)[0].astype(BF)
    term_down = dot_tn(slope_out, hidden).astype(BF)
    term_up = dot_tn(level_b, slope_pre).astype(BF)
    grads = scatter_rows((term_down, term_up))
    grad_coarse = upstream + scatter_cols(dot_nt(slope_pre, up_full))

    both = jnp.concatenate([coarse, grad_coarse], axis=1).astype(BF)
    quads = to_tile([both[k * 16 : (k + 1) * 16] for k in range(4)])
    both = jnp.stack(quads).reshape(2, 2, 4, 4, 2 * wide).transpose(0, 2, 1, 3, 4)
    both = both.reshape(tile_rows // 2, tile_cols // 2, 2 * wide).astype(F32)
    return (both[..., :wide], both[..., wide:], grads[1], grads[0].T)


def solution(mesh):
    finer = Mesh(
        mesh.devices.reshape(NX, NZ, NL, NCORE, mesh.shape["dp"]),
        ("xh", "z", "xl", "core", "dp"),
    )
    rows = ("dp", *ROWS)
    in_specs = (
        P(rows, COLS, None),
        P(),
        P(),
        P(),
        P(None, COLS),
        P(ROWS, COLS),
        P(COLS, ROWS),
        P(rows, COLS, None),
    )
    out_specs = (
        P(rows, COLS, None),
        P(rows, COLS, None),
        P(ROWS, ("dp", *COLS)),
        P(COLS, rows),
    )
    return jax.shard_map(
        whole_step, mesh=finer, in_specs=in_specs, out_specs=out_specs, check_vma=False
    )
```

```python
import jax
import jax.numpy as jnp
from jax import lax
from jax.experimental import pallas as pl
from jax.experimental.pallas import tpu as pltpu
from jax.sharding import Mesh
from jax.sharding import PartitionSpec as P


NX, NZ, NL, NCORE = 2, 8, 2, 2
ROWS = ("xh", "z")
COLS = ("xl", "core")
GRID = ("xh", "z", "xl", "core")
NROW, NCOL = NX * NZ, NL * NCORE

eps_norm = 1e-05
eps_unit = 1e-06
BF = jnp.bfloat16
F32 = jnp.float32


def dot(a, b):
    return jnp.dot(a, b, preferred_element_type=F32)


def dot_nt(a, b):
    return lax.dot_general(a, b, (((1,), (1,)), ((), ())), preferred_element_type=F32)


def dot_tn(a, b):
    return lax.dot_general(a, b, (((0,), (0,)), ((), ())), preferred_element_type=F32)


def layer_norm(value):
    average = jnp.mean(value, axis=-1, keepdims=True)
    centred = value - average
    spread = jnp.mean(centred * centred, axis=-1, keepdims=True)
    inverse = lax.rsqrt(spread + eps_norm)
    return (centred * inverse, inverse)


def norm_slope(upstream, normed, inverse):
    first_mean = jnp.mean(upstream, axis=-1, keepdims=True)
    second_mean = jnp.mean(upstream * normed, axis=-1, keepdims=True)
    return inverse * (upstream - first_mean - normed * second_mean)


def exact_gelu(value):
    return jax.nn.gelu(value, approximate=False)


def to_grid(array, dr, dc):
    pairs = [
        (r * NCOL + c, ((r + dr) % NROW) * NCOL + (c + dc) % NCOL)
        for r in range(NROW)
        for c in range(NCOL)
    ]
    return lax.ppermute(array, GRID, pairs)


def swap_core(array):
    return lax.ppermute(array, "core", [(0, 1), (1, 0)])


def swap_xl(array):
    return lax.ppermute(array, "xl", [(0, 1), (1, 0)])


def swap_half(array):
    return lax.ppermute(array, "xh", [(0, 1), (1, 0)])


def along_z(array, step):
    return lax.ppermute(array, "z", [(i, (i + step) % NZ) for i in range(NZ)])


def across_z(array, step):
    pairs = []
    for h in range(NX):
        for i in range(NZ):
            pairs.append((h * NZ + i, (1 - h) * NZ + (i + step) % NZ))
    return lax.ppermute(array, ROWS, pairs)


def gather_cols(rows):
    other = swap_xl(rows)
    near = jnp.concatenate([rows, other], axis=0)
    across = swap_core(near)
    return jnp.concatenate([near, across], axis=0)


def scatter_cols(rows):
    rows = rows.astype(BF)
    half, quarter = rows.shape[0] // 2, rows.shape[0] // 4
    near = rows[:half].astype(F32) + swap_core(rows[half:]).astype(F32)
    return near[:quarter] + swap_xl(near[quarter:].astype(BF)).astype(F32)


def gather_rows(shard):
    other = swap_half(shard)
    first = lax.axis_index("xh") == 0
    own = jnp.stack([jnp.where(first, shard, other), jnp.where(first, other, shard)])
    z = lax.axis_index("z")
    full = jnp.zeros((NX, NZ, *shard.shape), shard.dtype)

    def put(full, block, k):
        return lax.dynamic_update_slice_in_dim(full, block[:, None], (z + k) % NZ, 1)

    full = put(full, own, 0)
    left = right = own
    for k in (1, 2, 3):
        left, right = along_z(left, -1), along_z(right, 1)
        full = put(full, left, k)
        full = put(full, right, NZ - k)
    far = [along_z(left[0], -1), along_z(right[1], 1)]
    far = jnp.stack(far)
    return put(full, far, 4)


def scatter_rows(terms):
    blocks = [term.reshape(NX, NZ, -1, term.shape[-1]) for term in terms]
    z = lax.axis_index("z")

    def block(k):
        return jnp.stack([lax.dynamic_index_in_dim(b, (z + k) % NZ, 1, False) for b in blocks], 1)

    own = block(0)
    own_other = swap_half(jnp.where(lax.axis_index("xh") == 0, own[1], own[0]))
    far = block(4)
    left, right = along_z(far[0], -1), along_z(far[1], 1)
    near_left, near_right = block(NZ - 3), block(3)
    left = jnp.stack([near_left[0] + left, near_left[1]])
    right = jnp.stack([near_right[0], near_right[1] + right])
    for k in (2, 1):
        left, right = along_z(left, -1), along_z(right, 1)
        left, right = left + block(NZ - k), right + block(k)
    first = lax.axis_index("xh") == 0

    def mine(v):
        return jnp.where(first, v[0], v[1])

    def theirs(v):
        return jnp.where(first, v[1], v[0])

    near = [along_z(mine(left), -1), along_z(mine(right), 1)]
    cross = [across_z(theirs(left), -1), across_z(theirs(right), 1)]
    total = mine(own).astype(F32) + own_other.astype(F32)
    for part in near + cross:
        total = total + part.astype(F32)
    return total


def order_kernel(fields_ref, cot_ref, *outs):
    n = fields_ref.shape[0]
    to = lax.broadcasted_iota(jnp.int32, (n, n), 0)
    at = lax.broadcasted_iota(jnp.int32, (n, n), 1)
    c4, r4 = to & 3, (to >> 2) & 3
    pr, pc = (to >> 4) & 1, (to >> 5) & 1
    qb, qa = (to >> 6) & 1, (to >> 7) & 1
    source = (qa * 8 + r4 * 2 + pr) * 16 + qb * 8 + c4 * 2 + pc
    pick = jnp.where(at == source, 1.0, 0.0).astype(BF)
    moved = dot(pick, fields_ref[...].astype(BF)).astype(BF)
    m = cot_ref.shape[0]
    to = lax.broadcasted_iota(jnp.int32, (m, m), 0)
    at = lax.broadcasted_iota(jnp.int32, (m, m), 1)
    source = (((to >> 5) & 1) * 4 + ((to >> 2) & 3)) * 8 + ((to >> 4) & 1) * 4 + (to & 3)
    pick = jnp.where(at == source, 1.0, 0.0).astype(BF)
    cot = dot(pick, cot_ref[...]).astype(BF)
    wide = fields_ref.shape[1]
    for k in range(4):
        outs[k][:64] = moved[k * 64 : (k + 1) * 64]
        outs[k][64:80] = cot[k * 16 : (k + 1) * 16, :wide]
        outs[k][80:] = cot[k * 16 : (k + 1) * 16, wide:]


def window_kernel(scale_ref, x0, x1, x2, x3, qkv_ref, proj_ref, out_ref, cot_ref):
    quads = (x0[...], x1[...], x2[...], x3[...])
    x = jnp.concatenate([q[k * 16 : (k + 1) * 16] for k in range(4) for q in quads], axis=0)
    channels = x.shape[1]
    heads = channels // 64
    raw = dot(x, qkv_ref[...])
    mixed = []
    for h in range(heads):
        q = raw[:, h * 64 : (h + 1) * 64]
        k = raw[:, channels + h * 64 : channels + (h + 1) * 64]
        v = raw[:, 2 * channels + h * 64 : 2 * channels + (h + 1) * 64].astype(BF)
        q = q * lax.rsqrt(jnp.sum(q * q, axis=-1, keepdims=True) + eps_unit)
        k = k * lax.rsqrt(jnp.sum(k * k, axis=-1, keepdims=True) + eps_unit)
        scores = dot_nt(q.astype(BF), k.astype(BF))
        weights = jnp.exp(scores * scale_ref[h])
        total = jnp.sum(weights, axis=-1, keepdims=True)
        mixed.append(dot(weights.astype(BF), v) / total)
    mixed = jnp.concatenate(mixed, axis=1).astype(BF)
    normed, _ = layer_norm(dot(mixed, proj_ref[...]))
    stream = (x.astype(F32) + normed).astype(BF)
    own = stream.shape[0] // 4
    for k in range(4):
        out_ref[:, k * channels : (k + 1) * channels] = stream[k * own : (k + 1) * own]
        cot_ref[k * 16 : (k + 1) * 16, :channels] = quads[k][64:80]
        cot_ref[k * 16 : (k + 1) * 16, channels:] = quads[k][80:]


def level_kernel(merged_ref, own_ref, core_ref, near_ref, far_ref, level_ref, bf_ref):
    merged = merged_ref[...]
    parts = [dot_nt(merged, r[...]) for r in (own_ref, core_ref, near_ref, far_ref)]
    xl, core = lax.axis_index("xl") == 0, lax.axis_index("core") == 0
    low = [jnp.where(xl, parts[k], parts[k + 2]) for k in (0, 1)]
    high = [jnp.where(xl, parts[k + 2], parts[k]) for k in (0, 1)]
    ordered = []
    for pair in (low, high):
        ordered += [jnp.where(core, pair[0], pair[1]), jnp.where(core, pair[1], pair[0])]
    level, _ = layer_norm(jnp.concatenate(ordered, axis=1))
    level_ref[...] = level
    bf_ref[...] = level.astype(BF)


def in_vmem(array):
    return pltpu.with_memory_space_constraint(array, pltpu.VMEM)


def whole(count):
    return [pl.BlockSpec(memory_space=pltpu.VMEM)] * count


def whole_step(fields, logit_scale, w_qkv, w_proj, w_merge, w_up, w_down, cotangent):
    tile_rows, tile_cols, channels = fields.shape
    wide = cotangent.shape[-1]
    tokens = tile_rows * tile_cols
    own = tokens // 4

    tile_quads = pl.pallas_call(
        order_kernel,
        out_shape=[jax.ShapeDtypeStruct((96, channels), BF)] * 4,
        in_specs=whole(2),
        out_specs=whole(4),
        name="order",
    )(fields.reshape(tokens, channels), cotangent.reshape(own, wide))

    def to_window(quads):
        return (
            quads[3],
            to_grid(quads[2], 0, -1),
            to_grid(quads[1], -1, 0),
            to_grid(quads[0], -1, -1),
        )

    def to_tile(quads):
        return (
            to_grid(quads[3], 1, 1),
            to_grid(quads[2], 1, 0),
            to_grid(quads[1], 0, 1),
            quads[0],
        )

    x = to_window(tile_quads)

    weights = gather_rows(jnp.stack([w_up, w_down.T]))
    up_full = weights[:, :, 0].reshape(wide, -1)
    down_full = weights[:, :, 1].reshape(wide, -1)

    merge_own = w_merge.T
    merge_near = swap_xl(merge_own)
    merge_core = swap_core(merge_own)
    merge_far = swap_core(merge_near)

    merged, cot = pl.pallas_call(
        window_kernel,
        out_shape=[
            jax.ShapeDtypeStruct((own, 4 * channels), BF),
            jax.ShapeDtypeStruct((own, wide), BF),
        ],
        in_specs=[pl.BlockSpec(memory_space=pltpu.SMEM)] + whole(6),
        out_specs=whole(2),
        cost_estimate=pl.CostEstimate(
            flops=2 * tokens * channels * (4 * channels + 2 * tokens),
            transcendentals=tokens * tokens * 6,
            bytes_accessed=2_000_000,
        ),
        name="window",
    )(
        logit_scale,
        *x,
        in_vmem(w_qkv),
        in_vmem(w_proj),
    )
    level, level_own = pl.pallas_call(
        level_kernel,
        out_shape=[jax.ShapeDtypeStruct((own, wide), F32), jax.ShapeDtypeStruct((own, wide), BF)],
        in_specs=whole(5),
        out_specs=whole(2),
        cost_estimate=pl.CostEstimate(
            flops=8 * own * channels * wide, transcendentals=own, bytes_accessed=3_000_000
        ),
        name="level",
    )(merged, *(in_vmem(w) for w in (merge_own, merge_core, merge_near, merge_far)))
    level_b = gather_cols(level_own)

    hidden_pre = dot(level_b, up_full)
    hidden = exact_gelu(hidden_pre).astype(BF)

    branch_norm, branch_inv = layer_norm(scatter_cols(dot_nt(hidden, down_full)))
    coarse = level + branch_norm
    upstream = cot.astype(F32)
    slope_own = norm_slope(upstream, branch_norm, branch_inv).astype(BF)
    slope_out = gather_cols(slope_own)
    slope_hidden = dot(slope_out, down_full)
    _, pullback = jax.vjp(exact_gelu, hidden_pre)
    slope_pre = pullback(slope_hidden)[0].astype(BF)
    term_down = dot_tn(slope_out, hidden).astype(BF)
    term_up = dot_tn(level_b, slope_pre).astype(BF)
    grads = scatter_rows((term_down, term_up))
    grad_coarse = upstream + scatter_cols(dot_nt(slope_pre, up_full))

    both = jnp.concatenate([coarse, grad_coarse], axis=1).astype(BF)
    quads = to_tile([both[k * 16 : (k + 1) * 16] for k in range(4)])
    both = jnp.stack(quads).reshape(2, 2, 4, 4, 2 * wide).transpose(0, 2, 1, 3, 4)
    both = both.reshape(tile_rows // 2, tile_cols // 2, 2 * wide).astype(F32)
    return (both[..., :wide], both[..., wide:], grads[1], grads[0].T)


def solution(mesh):
    finer = Mesh(
        mesh.devices.reshape(NX, NZ, NL, NCORE, mesh.shape["dp"]),
        ("xh", "z", "xl", "core", "dp"),
    )
    rows = ("dp", *ROWS)
    in_specs = (
        P(rows, COLS, None),
        P(),
        P(),
        P(),
        P(None, COLS),
        P(ROWS, COLS),
        P(COLS, ROWS),
        P(rows, COLS, None),
    )
    out_specs = (
        P(rows, COLS, None),
        P(rows, COLS, None),
        P(ROWS, ("dp", *COLS)),
        P(COLS, rows),
    )
    return jax.shard_map(
        whole_step, mesh=finer, in_specs=in_specs, out_specs=out_specs, check_vma=False
    )
```

```python
import jax
import jax.numpy as jnp
from jax import lax
from jax.experimental import pallas as pl
from jax.experimental.pallas import tpu as pltpu
from jax.sharding import Mesh
from jax.sharding import PartitionSpec as P


NX, NZ, NL, NCORE = 2, 8, 2, 2
ROWS = ("xh", "z")
COLS = ("xl", "core")
GRID = ("xh", "z", "xl", "core")
NROW, NCOL = NX * NZ, NL * NCORE

eps_norm = 1e-05
eps_unit = 1e-06
BF = jnp.bfloat16
LIMIT = 24 * 2**20
F32 = jnp.float32


def dot(a, b):
    return jnp.dot(a, b, preferred_element_type=F32)


def dot_nt(a, b):
    return lax.dot_general(a, b, (((1,), (1,)), ((), ())), preferred_element_type=F32)


def dot_tn(a, b):
    return lax.dot_general(a, b, (((0,), (0,)), ((), ())), preferred_element_type=F32)


def layer_norm(value):
    average = jnp.mean(value, axis=-1, keepdims=True)
    centred = value - average
    spread = jnp.mean(centred * centred, axis=-1, keepdims=True)
    inverse = lax.rsqrt(spread + eps_norm)
    return (centred * inverse, inverse)


def norm_slope(upstream, normed, inverse):
    first_mean = jnp.mean(upstream, axis=-1, keepdims=True)
    second_mean = jnp.mean(upstream * normed, axis=-1, keepdims=True)
    return inverse * (upstream - first_mean - normed * second_mean)


def in_vmem(array):
    return pltpu.with_memory_space_constraint(array, pltpu.VMEM)


def vmem(shape, dtype):
    return pltpu.VMEM(shape, dtype)


def to_grid(array, dr, dc):
    pairs = [
        (r * NCOL + c, ((r + dr) % NROW) * NCOL + (c + dc) % NCOL)
        for r in range(NROW)
        for c in range(NCOL)
    ]
    return lax.ppermute(array, GRID, pairs)


def swap_core(array):
    return lax.ppermute(array, "core", [(0, 1), (1, 0)])


def swap_xl(array):
    return lax.ppermute(array, "xl", [(0, 1), (1, 0)])


def swap_half(array):
    return lax.ppermute(array, "xh", [(0, 1), (1, 0)])


def along_z(array, step):
    return lax.ppermute(array, "z", [(i, (i + step) % NZ) for i in range(NZ)])


def across_z(array, step):
    pairs = []
    for h in range(NX):
        for i in range(NZ):
            pairs.append((h * NZ + i, (1 - h) * NZ + (i + step) % NZ))
    return lax.ppermute(array, ROWS, pairs)


def gather_cols(rows):
    near = jnp.concatenate([rows, swap_xl(rows)], axis=0)
    return jnp.concatenate([near, swap_core(near)], axis=0)


def scatter_cols(low, high):
    quarter = low.shape[0] // 2
    near = low.astype(F32) + swap_core(high).astype(F32)
    return near[:quarter] + swap_xl(near[quarter:].astype(BF)).astype(F32)


def gather_rows(shard):
    other = swap_half(shard)
    own = pl.pallas_call(
        pair_kernel,
        out_shape=vmem((NX, *shard.shape), shard.dtype),
        in_specs=whole(2),
        out_specs=whole(1)[0],
        compiler_params=pltpu.CompilerParams(vmem_limit_bytes=LIMIT),
        name="pair",
    )(in_vmem(shard), in_vmem(other))
    pieces = [own]
    left = right = own
    for _ in range(3):
        left, right = along_z(left, -1), along_z(right, 1)
        pieces += [left, right]
    far = [along_z(left[0], -1), along_z(right[1], 1)]
    return pieces + far


def scatter_rows(terms):
    blocks = [term.reshape(NX, NZ, -1, term.shape[-1]) for term in terms]
    z = lax.axis_index("z")

    def block(k):
        return jnp.stack([lax.dynamic_index_in_dim(b, (z + k) % NZ, 1, False) for b in blocks], 1)

    own = block(0)
    own_other = swap_half(jnp.where(lax.axis_index("xh") == 0, own[1], own[0]))
    far = block(4)
    left, right = along_z(far[0], -1), along_z(far[1], 1)
    near_left, near_right = block(NZ - 3), block(3)
    left = jnp.stack([near_left[0] + left, near_left[1]])
    right = jnp.stack([near_right[0], near_right[1] + right])
    for k in (2, 1):
        left, right = along_z(left, -1), along_z(right, 1)
        left, right = left + block(NZ - k), right + block(k)
    first = lax.axis_index("xh") == 0

    def mine(v):
        return jnp.where(first, v[0], v[1])

    def theirs(v):
        return jnp.where(first, v[1], v[0])

    near = [along_z(mine(left), -1), along_z(mine(right), 1)]
    cross = [across_z(theirs(left), -1), across_z(theirs(right), 1)]
    total = mine(own).astype(F32) + own_other.astype(F32)
    for part in near + cross:
        total = total + part.astype(F32)
    return total


def pair_kernel(own_ref, other_ref, out_ref):
    first = lax.axis_index("xh") == 0
    out_ref[0] = jnp.where(first, own_ref[...], other_ref[...])
    out_ref[1] = jnp.where(first, other_ref[...], own_ref[...])


def forward_kernel(*refs):
    level, near, across = refs[:3]
    pieces = refs[3:10]
    far = refs[10:12]
    level_b, up, down, hidden_ref, slope_ref, low_ref, high_ref = refs[12:]
    own = level.shape[0]
    level_b[:own] = level[...]
    level_b[own : 2 * own] = near[...]
    level_b[2 * own :] = across[...]
    z = lax.axis_index("z")
    rows = pieces[0].shape[2]

    def put(piece, half, k):
        start = pl.multiple_of((half * NZ + lax.rem(z + k, NZ)) * rows, 16)
        up[pl.ds(start, rows), :] = piece[0]
        down[pl.ds(start, rows), :] = piece[1]

    for piece, k in zip(pieces, (0, 1, 7, 2, 6, 3, 5)):
        for half in (0, 1):
            put(piece[half], half, k)
    put(far[0][...], 0, 4)
    put(far[1][...], 1, 4)
    pre = dot(level_b[...], up[...])
    share = 0.5 + 0.5 * lax.erf(pre * 0.7071067811865476)
    slope_ref[...] = share + pre * (0.3989422804014327 * jnp.exp(-0.5 * pre * pre))
    hidden = (pre * share).astype(BF)
    hidden_ref[...] = hidden
    sums = dot_nt(hidden, down[...]).astype(BF)
    low_ref[...] = sums[: 2 * own]
    high_ref[...] = sums[2 * own :]


def order_kernel(fields_ref, cot_ref, *outs):
    n = fields_ref.shape[0]
    to = lax.broadcasted_iota(jnp.int32, (n, n), 0)
    at = lax.broadcasted_iota(jnp.int32, (n, n), 1)
    c4, r4 = to & 3, (to >> 2) & 3
    pr, pc = (to >> 4) & 1, (to >> 5) & 1
    qb, qa = (to >> 6) & 1, (to >> 7) & 1
    source = (qa * 8 + r4 * 2 + pr) * 16 + qb * 8 + c4 * 2 + pc
    pick = jnp.where(at == source, 1.0, 0.0).astype(BF)
    moved = dot(pick, fields_ref[...].astype(BF)).astype(BF)
    m = cot_ref.shape[0]
    to = lax.broadcasted_iota(jnp.int32, (m, m), 0)
    at = lax.broadcasted_iota(jnp.int32, (m, m), 1)
    source = (((to >> 5) & 1) * 4 + ((to >> 2) & 3)) * 8 + ((to >> 4) & 1) * 4 + (to & 3)
    pick = jnp.where(at == source, 1.0, 0.0).astype(BF)
    cot = dot(pick, cot_ref[...]).astype(BF)
    wide = fields_ref.shape[1]
    for k in range(4):
        outs[k][:64] = moved[k * 64 : (k + 1) * 64]
        outs[k][64:80] = cot[k * 16 : (k + 1) * 16, :wide]
        outs[k][80:] = cot[k * 16 : (k + 1) * 16, wide:]


def window_kernel(scale_ref, x0, x1, x2, x3, qkv_ref, proj_ref, out_ref, cot_ref):
    quads = (x0[...], x1[...], x2[...], x3[...])
    x = jnp.concatenate([q[k * 16 : (k + 1) * 16] for k in range(4) for q in quads], axis=0)
    channels = x.shape[1]
    heads = channels // 64
    raw = dot(x, qkv_ref[...])
    mixed = []
    for h in range(heads):
        q = raw[:, h * 64 : (h + 1) * 64]
        k = raw[:, channels + h * 64 : channels + (h + 1) * 64]
        v = raw[:, 2 * channels + h * 64 : 2 * channels + (h + 1) * 64].astype(BF)
        q = q * lax.rsqrt(jnp.sum(q * q, axis=-1, keepdims=True) + eps_unit)
        k = k * lax.rsqrt(jnp.sum(k * k, axis=-1, keepdims=True) + eps_unit)
        scores = dot_nt(q.astype(BF), k.astype(BF))
        weights = jnp.exp(scores * scale_ref[h])
        total = jnp.sum(weights, axis=-1, keepdims=True)
        mixed.append(dot(weights.astype(BF), v) / total)
    mixed = jnp.concatenate(mixed, axis=1).astype(BF)
    normed, _ = layer_norm(dot(mixed, proj_ref[...]))
    stream = (x.astype(F32) + normed).astype(BF)
    own = stream.shape[0] // 4
    for k in range(4):
        out_ref[:, k * channels : (k + 1) * channels] = stream[k * own : (k + 1) * own]
        cot_ref[k * 16 : (k + 1) * 16, :channels] = quads[k][64:80]
        cot_ref[k * 16 : (k + 1) * 16, channels:] = quads[k][80:]


def level_kernel(merged_ref, own_ref, core_ref, near_ref, far_ref, level_ref, bf_ref):
    merged = merged_ref[...]
    parts = [dot_nt(merged, r[...]) for r in (own_ref, core_ref, near_ref, far_ref)]
    xl, core = lax.axis_index("xl") == 0, lax.axis_index("core") == 0
    low = [jnp.where(xl, parts[k], parts[k + 2]) for k in (0, 1)]
    high = [jnp.where(xl, parts[k + 2], parts[k]) for k in (0, 1)]
    ordered = []
    for pair in (low, high):
        ordered += [jnp.where(core, pair[0], pair[1]), jnp.where(core, pair[1], pair[0])]
    level, _ = layer_norm(jnp.concatenate(ordered, axis=1))
    level_ref[...] = level
    bf_ref[...] = level.astype(BF)


def whole(count):
    return [pl.BlockSpec(memory_space=pltpu.VMEM)] * count


def whole_step(fields, logit_scale, w_qkv, w_proj, w_merge, w_up, w_down, cotangent):
    tile_rows, tile_cols, channels = fields.shape
    wide = cotangent.shape[-1]
    tokens = tile_rows * tile_cols
    own = tokens // 4

    tile_quads = pl.pallas_call(
        order_kernel,
        out_shape=[vmem((96, channels), BF)] * 4,
        in_specs=whole(2),
        out_specs=whole(4),
        compiler_params=pltpu.CompilerParams(vmem_limit_bytes=LIMIT),
        name="order",
    )(fields.reshape(tokens, channels), cotangent.reshape(own, wide))

    def to_window(quads):
        return (
            quads[3],
            to_grid(quads[2], 0, -1),
            to_grid(quads[1], -1, 0),
            to_grid(quads[0], -1, -1),
        )

    def to_tile(quads):
        return (
            to_grid(quads[3], 1, 1),
            to_grid(quads[2], 1, 0),
            to_grid(quads[1], 0, 1),
            quads[0],
        )

    x = to_window(tile_quads)

    weights = gather_rows(jnp.stack([w_up, w_down.T]))
    merge_own = w_merge.T
    merge_near = swap_xl(merge_own)
    merge_core = swap_core(merge_own)
    merge_far = swap_core(merge_near)

    merged, cot = pl.pallas_call(
        window_kernel,
        out_shape=[
            vmem((own, 4 * channels), BF),
            vmem((own, wide), BF),
        ],
        in_specs=[pl.BlockSpec(memory_space=pltpu.SMEM)] + whole(6),
        out_specs=whole(2),
        cost_estimate=pl.CostEstimate(
            flops=2 * tokens * channels * (4 * channels + 2 * tokens),
            transcendentals=tokens * tokens * 6,
            bytes_accessed=2_000_000,
        ),
        compiler_params=pltpu.CompilerParams(vmem_limit_bytes=LIMIT),
        name="window",
    )(
        logit_scale,
        *(in_vmem(q) for q in x),
        in_vmem(w_qkv),
        in_vmem(w_proj),
    )
    level, level_own = pl.pallas_call(
        level_kernel,
        out_shape=[vmem((own, wide), F32), vmem((own, wide), BF)],
        in_specs=whole(5),
        out_specs=whole(2),
        cost_estimate=pl.CostEstimate(
            flops=8 * own * channels * wide, transcendentals=own, bytes_accessed=3_000_000
        ),
        compiler_params=pltpu.CompilerParams(vmem_limit_bytes=LIMIT),
        name="level",
    )(in_vmem(merged), *(in_vmem(w) for w in (merge_own, merge_core, merge_near, merge_far)))
    level_near = swap_xl(level_own)
    level_across = swap_core(jnp.concatenate([level_own, level_near], axis=0))
    hid = w_up.shape[1]
    level_b, up_full, down_full, hidden, gelu_slope, low, high = pl.pallas_call(
        forward_kernel,
        out_shape=[
            vmem((tokens, wide), BF),
            vmem((wide, hid), BF),
            vmem((wide, hid), BF),
            vmem((tokens, hid), BF),
            vmem((tokens, hid), F32),
            vmem((2 * own, wide), BF),
            vmem((2 * own, wide), BF),
        ],
        in_specs=whole(12),
        out_specs=whole(7),
        cost_estimate=pl.CostEstimate(
            flops=4 * tokens * wide * hid, transcendentals=2 * tokens * hid, bytes_accessed=6_000_000
        ),
        compiler_params=pltpu.CompilerParams(vmem_limit_bytes=LIMIT),
        name="forward",
    )(*(in_vmem(v) for v in (level_own, level_near, level_across, *weights)))

    branch_norm, branch_inv = layer_norm(scatter_cols(low, high))
    coarse = level + branch_norm
    upstream = cot.astype(F32)
    slope_own = norm_slope(upstream, branch_norm, branch_inv).astype(BF)
    slope_out = gather_cols(slope_own)
    slope_pre = (gelu_slope * dot(slope_out, down_full)).astype(BF)
    term_down = dot_tn(slope_out, hidden).astype(BF)
    term_up = dot_tn(level_b, slope_pre).astype(BF)
    grads = scatter_rows((term_down, term_up))
    sums = dot_nt(slope_pre, up_full).astype(BF)
    grad_coarse = upstream + scatter_cols(sums[: 2 * own], sums[2 * own :])

    both = jnp.concatenate([coarse, grad_coarse], axis=1).astype(BF)
    quads = to_tile([both[k * 16 : (k + 1) * 16] for k in range(4)])
    both = jnp.stack(quads).reshape(2, 2, 4, 4, 2 * wide).transpose(0, 2, 1, 3, 4)
    both = both.reshape(tile_rows // 2, tile_cols // 2, 2 * wide).astype(F32)
    return (both[..., :wide], both[..., wide:], grads[1], grads[0].T)


def solution(mesh):
    finer = Mesh(
        mesh.devices.reshape(NX, NZ, NL, NCORE, mesh.shape["dp"]),
        ("xh", "z", "xl", "core", "dp"),
    )
    rows = ("dp", *ROWS)
    in_specs = (
        P(rows, COLS, None),
        P(),
        P(),
        P(),
        P(None, COLS),
        P(ROWS, COLS),
        P(COLS, ROWS),
        P(rows, COLS, None),
    )
    out_specs = (
        P(rows, COLS, None),
        P(rows, COLS, None),
        P(ROWS, ("dp", *COLS)),
        P(COLS, rows),
    )
    return jax.shard_map(
        whole_step, mesh=finer, in_specs=in_specs, out_specs=out_specs, check_vma=False
    )
```

```python
import jax
import jax.numpy as jnp
from jax import lax
from jax.experimental import pallas as pl
from jax.experimental.pallas import tpu as pltpu
from jax.sharding import Mesh
from jax.sharding import PartitionSpec as P


NX, NZ, NL, NCORE = 2, 8, 2, 2
ROWS = ("xh", "z")
COLS = ("xl", "core")
GRID = ("xh", "z", "xl", "core")
NROW, NCOL = NX * NZ, NL * NCORE

eps_norm = 1e-05
eps_unit = 1e-06
BF = jnp.bfloat16
LIMIT = 24 * 2**20
F32 = jnp.float32


def dot(a, b):
    return jnp.dot(a, b, preferred_element_type=F32)


def dot_nt(a, b):
    return lax.dot_general(a, b, (((1,), (1,)), ((), ())), preferred_element_type=F32)


def dot_tn(a, b):
    return lax.dot_general(a, b, (((0,), (0,)), ((), ())), preferred_element_type=F32)


def layer_norm(value):
    average = jnp.mean(value, axis=-1, keepdims=True)
    centred = value - average
    spread = jnp.mean(centred * centred, axis=-1, keepdims=True)
    inverse = lax.rsqrt(spread + eps_norm)
    return (centred * inverse, inverse)


def norm_slope(upstream, normed, inverse):
    first_mean = jnp.mean(upstream, axis=-1, keepdims=True)
    second_mean = jnp.mean(upstream * normed, axis=-1, keepdims=True)
    return inverse * (upstream - first_mean - normed * second_mean)


def in_vmem(array):
    return pltpu.with_memory_space_constraint(array, pltpu.VMEM)


def vmem(shape, dtype):
    return pltpu.VMEM(shape, dtype)


def to_grid(array, dr, dc):
    pairs = [
        (r * NCOL + c, ((r + dr) % NROW) * NCOL + (c + dc) % NCOL)
        for r in range(NROW)
        for c in range(NCOL)
    ]
    return lax.ppermute(array, GRID, pairs)


def swap_core(array):
    return lax.ppermute(array, "core", [(0, 1), (1, 0)])


def swap_xl(array):
    return lax.ppermute(array, "xl", [(0, 1), (1, 0)])


def swap_half(array):
    return lax.ppermute(array, "xh", [(0, 1), (1, 0)])


def along_z(array, step):
    return lax.ppermute(array, "z", [(i, (i + step) % NZ) for i in range(NZ)])


def across_z(array, step):
    pairs = []
    for h in range(NX):
        for i in range(NZ):
            pairs.append((h * NZ + i, (1 - h) * NZ + (i + step) % NZ))
    return lax.ppermute(array, ROWS, pairs)


def scatter_cols(low, high):
    quarter = low.shape[0] // 2
    near = low.astype(F32) + swap_core(high).astype(F32)
    return near[:quarter] + swap_xl(near[quarter:].astype(BF)).astype(F32)


def gather_rows(shard):
    other = swap_half(shard)
    own = pl.pallas_call(
        pair_kernel,
        out_shape=vmem((NX, *shard.shape), shard.dtype),
        in_specs=whole(2),
        out_specs=whole(1)[0],
        compiler_params=pltpu.CompilerParams(vmem_limit_bytes=LIMIT),
        name="pair",
    )(in_vmem(shard), in_vmem(other))
    pieces = [own]
    left = right = own
    for _ in range(3):
        left, right = along_z(left, -1), along_z(right, 1)
        pieces += [left, right]
    far = [along_z(left[0], -1), along_z(right[1], 1)]
    return pieces + far


def scatter_rows(terms):
    blocks = [term.reshape(NX, NZ, -1, term.shape[-1]) for term in terms]
    z = lax.axis_index("z")

    def block(k):
        return jnp.stack([lax.dynamic_index_in_dim(b, (z + k) % NZ, 1, False) for b in blocks], 1)

    own = block(0)
    own_other = swap_half(jnp.where(lax.axis_index("xh") == 0, own[1], own[0]))
    far = block(4)
    left, right = along_z(far[0], -1), along_z(far[1], 1)
    near_left, near_right = block(NZ - 3), block(3)
    left = jnp.stack([near_left[0] + left, near_left[1]])
    right = jnp.stack([near_right[0], near_right[1] + right])
    for k in (2, 1):
        left, right = along_z(left, -1), along_z(right, 1)
        left, right = left + block(NZ - k), right + block(k)
    first = lax.axis_index("xh") == 0

    def mine(v):
        return jnp.where(first, v[0], v[1])

    def theirs(v):
        return jnp.where(first, v[1], v[0])

    near = [along_z(mine(left), -1), along_z(mine(right), 1)]
    cross = [across_z(theirs(left), -1), across_z(theirs(right), 1)]
    shape = jax.ShapeDtypeStruct(own.shape[2:], F32)
    return pl.pallas_call(
        finish_kernel,
        out_shape=[shape] * 2,
        in_specs=whole(6),
        out_specs=whole(2),
        compiler_params=pltpu.CompilerParams(vmem_limit_bytes=LIMIT),
        name="finish",
    )(*(in_vmem(v) for v in (mine(own), own_other, *near, *cross)))


def pair_kernel(own_ref, other_ref, out_ref):
    first = lax.axis_index("xh") == 0
    out_ref[0] = jnp.where(first, own_ref[...], other_ref[...])
    out_ref[1] = jnp.where(first, other_ref[...], own_ref[...])


def forward_kernel(*refs):
    level, near, across = refs[:3]
    pieces = refs[3:10]
    far = refs[10:12]
    level_b, up, down, hidden_ref, slope_ref, low_ref, high_ref = refs[12:]
    own = level.shape[0]
    level_b[:own] = level[...]
    level_b[own : 2 * own] = near[...]
    level_b[2 * own :] = across[...]
    z = lax.axis_index("z")
    rows = pieces[0].shape[2]

    def put(piece, half, k):
        start = pl.multiple_of((half * NZ + lax.rem(z + k, NZ)) * rows, 16)
        up[pl.ds(start, rows), :] = piece[0]
        down[pl.ds(start, rows), :] = piece[1]

    for piece, k in zip(pieces, (0, 1, 7, 2, 6, 3, 5)):
        for half in (0, 1):
            put(piece[half], half, k)
    put(far[0][...], 0, 4)
    put(far[1][...], 1, 4)
    pre = dot(level_b[...], up[...])
    share = 0.5 + 0.5 * lax.erf(pre * 0.7071067811865476)
    slope_ref[...] = share + pre * (0.3989422804014327 * jnp.exp(-0.5 * pre * pre))
    hidden = (pre * share).astype(BF)
    hidden_ref[...] = hidden
    sums = dot_nt(hidden, down[...]).astype(BF)
    low_ref[...] = sums[: 2 * own]
    high_ref[...] = sums[2 * own :]


def backward_kernel(*refs):
    own_ref, near, across, level_b, up, down, hidden, gelu_slope = refs[:8]
    down_term, up_term, low_ref, high_ref, slope = refs[8:]
    own = own_ref.shape[0]
    slope[:own] = own_ref[...]
    slope[own : 2 * own] = near[...]
    slope[2 * own :] = across[...]
    down_term[...] = dot_tn(slope[...], hidden[...]).astype(BF)
    pre = (gelu_slope[...] * dot(slope[...], down[...])).astype(BF)
    up_term[...] = dot_tn(level_b[...], pre).astype(BF)
    sums = dot_nt(pre, up[...]).astype(BF)
    low_ref[...] = sums[: 2 * own]
    high_ref[...] = sums[2 * own :]


def finish_kernel(*refs):
    total = refs[0][...].astype(F32)
    for part in refs[1:-2]:
        total = total + part[...].astype(F32)
    refs[-2][...] = total[0]
    refs[-1][...] = total[1]


def order_kernel(fields_ref, cot_ref, *outs):
    n = fields_ref.shape[0]
    to = lax.broadcasted_iota(jnp.int32, (n, n), 0)
    at = lax.broadcasted_iota(jnp.int32, (n, n), 1)
    c4, r4 = to & 3, (to >> 2) & 3
    pr, pc = (to >> 4) & 1, (to >> 5) & 1
    qb, qa = (to >> 6) & 1, (to >> 7) & 1
    source = (qa * 8 + r4 * 2 + pr) * 16 + qb * 8 + c4 * 2 + pc
    pick = jnp.where(at == source, 1.0, 0.0).astype(BF)
    moved = dot(pick, fields_ref[...].astype(BF)).astype(BF)
    m = cot_ref.shape[0]
    to = lax.broadcasted_iota(jnp.int32, (m, m), 0)
    at = lax.broadcasted_iota(jnp.int32, (m, m), 1)
    source = (((to >> 5) & 1) * 4 + ((to >> 2) & 3)) * 8 + ((to >> 4) & 1) * 4 + (to & 3)
    pick = jnp.where(at == source, 1.0, 0.0).astype(BF)
    cot = dot(pick, cot_ref[...]).astype(BF)
    wide = fields_ref.shape[1]
    for k in range(4):
        outs[k][:64] = moved[k * 64 : (k + 1) * 64]
        outs[k][64:80] = cot[k * 16 : (k + 1) * 16, :wide]
        outs[k][80:] = cot[k * 16 : (k + 1) * 16, wide:]


def window_kernel(scale_ref, x0, x1, x2, x3, qkv_ref, proj_ref, out_ref, cot_ref):
    quads = (x0[...], x1[...], x2[...], x3[...])
    x = jnp.concatenate([q[k * 16 : (k + 1) * 16] for k in range(4) for q in quads], axis=0)
    channels = x.shape[1]
    heads = channels // 64
    raw = dot(x, qkv_ref[...])
    mixed = []
    for h in range(heads):
        q = raw[:, h * 64 : (h + 1) * 64]
        k = raw[:, channels + h * 64 : channels + (h + 1) * 64]
        v = raw[:, 2 * channels + h * 64 : 2 * channels + (h + 1) * 64].astype(BF)
        q = q * lax.rsqrt(jnp.sum(q * q, axis=-1, keepdims=True) + eps_unit)
        k = k * lax.rsqrt(jnp.sum(k * k, axis=-1, keepdims=True) + eps_unit)
        scores = dot_nt(q.astype(BF), k.astype(BF))
        weights = jnp.exp(scores * scale_ref[h])
        total = jnp.sum(weights, axis=-1, keepdims=True)
        mixed.append(dot(weights.astype(BF), v) / total)
    mixed = jnp.concatenate(mixed, axis=1).astype(BF)
    normed, _ = layer_norm(dot(mixed, proj_ref[...]))
    stream = (x.astype(F32) + normed).astype(BF)
    own = stream.shape[0] // 4
    for k in range(4):
        out_ref[:, k * channels : (k + 1) * channels] = stream[k * own : (k + 1) * own]
        cot_ref[k * 16 : (k + 1) * 16, :channels] = quads[k][64:80]
        cot_ref[k * 16 : (k + 1) * 16, channels:] = quads[k][80:]


def level_kernel(merged_ref, own_ref, core_ref, near_ref, far_ref, level_ref, bf_ref):
    merged = merged_ref[...]
    parts = [dot_nt(merged, r[...]) for r in (own_ref, core_ref, near_ref, far_ref)]
    xl, core = lax.axis_index("xl") == 0, lax.axis_index("core") == 0
    low = [jnp.where(xl, parts[k], parts[k + 2]) for k in (0, 1)]
    high = [jnp.where(xl, parts[k + 2], parts[k]) for k in (0, 1)]
    ordered = []
    for pair in (low, high):
        ordered += [jnp.where(core, pair[0], pair[1]), jnp.where(core, pair[1], pair[0])]
    level, _ = layer_norm(jnp.concatenate(ordered, axis=1))
    level_ref[...] = level
    bf_ref[...] = level.astype(BF)


def whole(count):
    return [pl.BlockSpec(memory_space=pltpu.VMEM)] * count


def whole_step(fields, logit_scale, w_qkv, w_proj, w_merge, w_up, w_down, cotangent):
    tile_rows, tile_cols, channels = fields.shape
    wide = cotangent.shape[-1]
    tokens = tile_rows * tile_cols
    own = tokens // 4

    tile_quads = pl.pallas_call(
        order_kernel,
        out_shape=[vmem((96, channels), BF)] * 4,
        in_specs=whole(2),
        out_specs=whole(4),
        compiler_params=pltpu.CompilerParams(vmem_limit_bytes=LIMIT),
        name="order",
    )(fields.reshape(tokens, channels), cotangent.reshape(own, wide))

    def to_window(quads):
        return (
            quads[3],
            to_grid(quads[2], 0, -1),
            to_grid(quads[1], -1, 0),
            to_grid(quads[0], -1, -1),
        )

    def to_tile(quads):
        return (
            to_grid(quads[3], 1, 1),
            to_grid(quads[2], 1, 0),
            to_grid(quads[1], 0, 1),
            quads[0],
        )

    x = to_window(tile_quads)

    weights = gather_rows(jnp.stack([w_up, w_down.T]))
    merge_own = w_merge.T
    merge_near = swap_xl(merge_own)
    merge_core = swap_core(merge_own)
    merge_far = swap_core(merge_near)

    merged, cot = pl.pallas_call(
        window_kernel,
        out_shape=[
            vmem((own, 4 * channels), BF),
            vmem((own, wide), BF),
        ],
        in_specs=[pl.BlockSpec(memory_space=pltpu.SMEM)] + whole(6),
        out_specs=whole(2),
        cost_estimate=pl.CostEstimate(
            flops=2 * tokens * channels * (4 * channels + 2 * tokens),
            transcendentals=tokens * tokens * 6,
            bytes_accessed=2_000_000,
        ),
        compiler_params=pltpu.CompilerParams(vmem_limit_bytes=LIMIT),
        name="window",
    )(
        logit_scale,
        *(in_vmem(q) for q in x),
        in_vmem(w_qkv),
        in_vmem(w_proj),
    )
    level, level_own = pl.pallas_call(
        level_kernel,
        out_shape=[vmem((own, wide), F32), vmem((own, wide), BF)],
        in_specs=whole(5),
        out_specs=whole(2),
        cost_estimate=pl.CostEstimate(
            flops=8 * own * channels * wide, transcendentals=own, bytes_accessed=3_000_000
        ),
        compiler_params=pltpu.CompilerParams(vmem_limit_bytes=LIMIT),
        name="level",
    )(in_vmem(merged), *(in_vmem(w) for w in (merge_own, merge_core, merge_near, merge_far)))
    level_near = swap_xl(level_own)
    level_across = swap_core(jnp.concatenate([level_own, level_near], axis=0))
    hid = w_up.shape[1]
    level_b, up_full, down_full, hidden, gelu_slope, low, high = pl.pallas_call(
        forward_kernel,
        out_shape=[
            vmem((tokens, wide), BF),
            vmem((wide, hid), BF),
            vmem((wide, hid), BF),
            vmem((tokens, hid), BF),
            vmem((tokens, hid), F32),
            vmem((2 * own, wide), BF),
            vmem((2 * own, wide), BF),
        ],
        in_specs=whole(12),
        out_specs=whole(7),
        cost_estimate=pl.CostEstimate(
            flops=4 * tokens * wide * hid, transcendentals=2 * tokens * hid, bytes_accessed=6_000_000
        ),
        compiler_params=pltpu.CompilerParams(vmem_limit_bytes=LIMIT),
        name="forward",
    )(*(in_vmem(v) for v in (level_own, level_near, level_across, *weights)))

    branch_norm, branch_inv = layer_norm(scatter_cols(low, high))
    coarse = level + branch_norm
    upstream = cot.astype(F32)
    slope_own = norm_slope(upstream, branch_norm, branch_inv).astype(BF)
    slope_near = swap_xl(slope_own)
    slope_across = swap_core(jnp.concatenate([slope_own, slope_near], axis=0))
    term_down, term_up, low, high = pl.pallas_call(
        backward_kernel,
        out_shape=[
            vmem((wide, hid), BF),
            vmem((wide, hid), BF),
            vmem((2 * own, wide), BF),
            vmem((2 * own, wide), BF),
        ],
        in_specs=whole(8),
        out_specs=whole(4),
        scratch_shapes=[pltpu.VMEM((tokens, wide), BF)],
        cost_estimate=pl.CostEstimate(
            flops=8 * tokens * wide * hid, transcendentals=0, bytes_accessed=6_000_000
        ),
        compiler_params=pltpu.CompilerParams(vmem_limit_bytes=LIMIT),
        name="backward",
    )(
        *(
            in_vmem(v)
            for v in (
                slope_own,
                slope_near,
                slope_across,
                level_b,
                up_full,
                down_full,
                hidden,
                gelu_slope,
            )
        )
    )
    grad_down, grad_up = scatter_rows((term_down, term_up))
    grad_coarse = upstream + scatter_cols(low, high)

    both = jnp.concatenate([coarse, grad_coarse], axis=1).astype(BF)
    quads = to_tile([both[k * 16 : (k + 1) * 16] for k in range(4)])
    both = jnp.stack(quads).reshape(2, 2, 4, 4, 2 * wide).transpose(0, 2, 1, 3, 4)
    both = both.reshape(tile_rows // 2, tile_cols // 2, 2 * wide).astype(F32)
    return (both[..., :wide], both[..., wide:], grad_up, grad_down.T)


def solution(mesh):
    finer = Mesh(
        mesh.devices.reshape(NX, NZ, NL, NCORE, mesh.shape["dp"]),
        ("xh", "z", "xl", "core", "dp"),
    )
    rows = ("dp", *ROWS)
    in_specs = (
        P(rows, COLS, None),
        P(),
        P(),
        P(),
        P(None, COLS),
        P(ROWS, COLS),
        P(COLS, ROWS),
        P(rows, COLS, None),
    )
    out_specs = (
        P(rows, COLS, None),
        P(rows, COLS, None),
        P(ROWS, ("dp", *COLS)),
        P(COLS, rows),
    )
    return jax.shard_map(
        whole_step, mesh=finer, in_specs=in_specs, out_specs=out_specs, check_vma=False
    )
```

```python
import jax
import jax.numpy as jnp
from jax import lax
from jax.experimental import pallas as pl
from jax.experimental.pallas import tpu as pltpu
from jax.sharding import Mesh
from jax.sharding import PartitionSpec as P


NX, NZ, NL, NCORE = 2, 8, 2, 2
ROWS = ("xh", "z")
COLS = ("xl", "core")
GRID = ("xh", "z", "xl", "core")
NROW, NCOL = NX * NZ, NL * NCORE

eps_norm = 1e-05
eps_unit = 1e-06
BF = jnp.bfloat16
LIMIT = 24 * 2**20
F32 = jnp.float32


def dot(a, b):
    return jnp.dot(a, b, preferred_element_type=F32)


def dot_nt(a, b):
    return lax.dot_general(a, b, (((1,), (1,)), ((), ())), preferred_element_type=F32)


def dot_tn(a, b):
    return lax.dot_general(a, b, (((0,), (0,)), ((), ())), preferred_element_type=F32)


def layer_norm(value):
    average = jnp.mean(value, axis=-1, keepdims=True)
    centred = value - average
    spread = jnp.mean(centred * centred, axis=-1, keepdims=True)
    inverse = lax.rsqrt(spread + eps_norm)
    return (centred * inverse, inverse)


def norm_slope(upstream, normed, inverse):
    first_mean = jnp.mean(upstream, axis=-1, keepdims=True)
    second_mean = jnp.mean(upstream * normed, axis=-1, keepdims=True)
    return inverse * (upstream - first_mean - normed * second_mean)


def in_vmem(array):
    return pltpu.with_memory_space_constraint(array, pltpu.VMEM)


def vmem(shape, dtype):
    return pltpu.VMEM(shape, dtype)


def to_grid(array, dr, dc):
    pairs = [
        (r * NCOL + c, ((r + dr) % NROW) * NCOL + (c + dc) % NCOL)
        for r in range(NROW)
        for c in range(NCOL)
    ]
    return lax.ppermute(array, GRID, pairs)


def swap_core(array):
    return lax.ppermute(array, "core", [(0, 1), (1, 0)])


def swap_xl(array):
    return lax.ppermute(array, "xl", [(0, 1), (1, 0)])


def swap_half(array):
    return lax.ppermute(array, "xh", [(0, 1), (1, 0)])


def along_z(array, step):
    return lax.ppermute(array, "z", [(i, (i + step) % NZ) for i in range(NZ)])


def across_z(array, step):
    pairs = []
    for h in range(NX):
        for i in range(NZ):
            pairs.append((h * NZ + i, (1 - h) * NZ + (i + step) % NZ))
    return lax.ppermute(array, ROWS, pairs)


def scatter_cols(low, high):
    quarter = low.shape[0] // 2
    near = low.astype(F32) + swap_core(high).astype(F32)
    far = swap_xl(near[quarter:].astype(BF))
    return near[:quarter] + far.astype(F32)


def gather_rows(shard):
    other = swap_half(shard)
    own = pl.pallas_call(
        pair_kernel,
        out_shape=vmem((NX, *shard.shape), shard.dtype),
        in_specs=whole(2),
        out_specs=whole(1)[0],
        compiler_params=pltpu.CompilerParams(vmem_limit_bytes=LIMIT),
        name="pair",
    )(in_vmem(shard), in_vmem(other))
    pieces = [own]
    left = right = own
    for _ in range(3):
        left, right = along_z(left, -1), along_z(right, 1)
        pieces += [left, right]
    far = [along_z(left[0], -1), along_z(right[1], 1)]
    return pieces + far


def scatter_rows(terms):
    apart = lax.optimization_barrier(terms)

    def block(k):
        return (terms if k < 5 else apart)[k]

    own, far = block(0), block(4)
    own_other = swap_half(own[1])
    left, right = along_z(far[0], -1), along_z(far[1], 1)
    near_left, near_right = block(NZ - 3), block(3)
    left = jnp.stack([near_left[0] + left, near_left[1]])
    right = jnp.stack([near_right[0], near_right[1] + right])
    for k in (2, 1):
        left, right = along_z(left, -1), along_z(right, 1)
        left, right = left + block(NZ - k), right + block(k)
    near = [along_z(left[0], -1), along_z(right[0], 1)]
    cross = [across_z(left[1], -1), across_z(right[1], 1)]
    shape = jax.ShapeDtypeStruct(own.shape[2:], F32)
    return pl.pallas_call(
        finish_kernel,
        out_shape=[shape] * 2,
        in_specs=whole(6),
        out_specs=whole(2),
        compiler_params=pltpu.CompilerParams(vmem_limit_bytes=LIMIT),
        name="finish",
    )(*(in_vmem(v) for v in (own[0], own_other, *near, *cross)))


def pair_kernel(own_ref, other_ref, out_ref):
    first = lax.axis_index("xh") == 0
    out_ref[0] = jnp.where(first, own_ref[...], other_ref[...])
    out_ref[1] = jnp.where(first, other_ref[...], own_ref[...])


def forward_kernel(*refs):
    level, near, across = refs[:3]
    pieces = refs[3:10]
    far = refs[10:12]
    level_b, up, down, hidden_ref, slope_ref, low_ref, high_ref = refs[12:]
    own = level.shape[0]
    level_b[:own] = level[...]
    level_b[own : 2 * own] = near[...]
    level_b[2 * own :] = across[...]
    z = lax.axis_index("z")
    rows = pieces[0].shape[2]

    def put(piece, half, k):
        start = pl.multiple_of((half * NZ + lax.rem(z + k, NZ)) * rows, 16)
        up[pl.ds(start, rows), :] = piece[0]
        down[pl.ds(start, rows), :] = piece[1]

    for piece, k in zip(pieces, (0, 1, 7, 2, 6, 3, 5)):
        for half in (0, 1):
            put(piece[half], half, k)
    put(far[0][...], 0, 4)
    put(far[1][...], 1, 4)
    pre = dot(level_b[...], up[...])
    share = 0.5 + 0.5 * lax.erf(pre * 0.7071067811865476)
    slope_ref[...] = share + pre * (0.3989422804014327 * jnp.exp(-0.5 * pre * pre))
    hidden = (pre * share).astype(BF)
    hidden_ref[...] = hidden
    sums = dot_nt(hidden, down[...]).astype(BF)
    low_ref[...] = sums[: 2 * own]
    high_ref[...] = sums[2 * own :]


def backward_kernel(*refs):
    own_ref, near, across, level_b, up, down, hidden, gelu_slope = refs[:8]
    terms, low_ref, high_ref, slope = refs[8:]
    own = own_ref.shape[0]
    slope[:own] = own_ref[...]
    slope[own : 2 * own] = near[...]
    slope[2 * own :] = across[...]
    z, xh = lax.axis_index("z"), lax.axis_index("xh")
    rows = terms.shape[3]

    def put(term, which):
        for half in range(NX):
            for at in range(NZ):
                start = (half * NZ + at) * rows
                block = term[start : start + rows]
                terms[lax.rem(at + NZ - z, NZ), lax.rem(half + xh, NX), which] = block

    put(dot_tn(slope[...], hidden[...]).astype(BF), 0)
    pre = (gelu_slope[...] * dot(slope[...], down[...])).astype(BF)
    put(dot_tn(level_b[...], pre).astype(BF), 1)
    sums = dot_nt(pre, up[...]).astype(BF)
    low_ref[...] = sums[: 2 * own]
    high_ref[...] = sums[2 * own :]


def finish_kernel(*refs):
    total = refs[0][...].astype(F32)
    for part in refs[1:-2]:
        total = total + part[...].astype(F32)
    refs[-2][...] = total[0]
    refs[-1][...] = total[1]


def order_kernel(fields_ref, cot_ref, *outs):
    n = fields_ref.shape[0]
    to = lax.broadcasted_iota(jnp.int32, (n, n), 0)
    at = lax.broadcasted_iota(jnp.int32, (n, n), 1)
    c4, r4 = to & 3, (to >> 2) & 3
    pr, pc = (to >> 4) & 1, (to >> 5) & 1
    qb, qa = (to >> 6) & 1, (to >> 7) & 1
    source = (qa * 8 + r4 * 2 + pr) * 16 + qb * 8 + c4 * 2 + pc
    pick = jnp.where(at == source, 1.0, 0.0).astype(BF)
    moved = dot(pick, fields_ref[...].astype(BF)).astype(BF)
    m = cot_ref.shape[0]
    to = lax.broadcasted_iota(jnp.int32, (m, m), 0)
    at = lax.broadcasted_iota(jnp.int32, (m, m), 1)
    source = (((to >> 5) & 1) * 4 + ((to >> 2) & 3)) * 8 + ((to >> 4) & 1) * 4 + (to & 3)
    pick = jnp.where(at == source, 1.0, 0.0).astype(BF)
    cot = dot(pick, cot_ref[...]).astype(BF)
    wide = fields_ref.shape[1]
    for k in range(4):
        outs[k][:64] = moved[k * 64 : (k + 1) * 64]
        outs[k][64:80] = cot[k * 16 : (k + 1) * 16, :wide]
        outs[k][80:] = cot[k * 16 : (k + 1) * 16, wide:]


def window_kernel(scale_ref, x0, x1, x2, x3, qkv_ref, proj_ref, out_ref, cot_ref):
    quads = (x0[...], x1[...], x2[...], x3[...])
    x = jnp.concatenate([q[k * 16 : (k + 1) * 16] for k in range(4) for q in quads], axis=0)
    channels = x.shape[1]
    heads = channels // 64
    raw = dot(x, qkv_ref[...])
    mixed = []
    for h in range(heads):
        q = raw[:, h * 64 : (h + 1) * 64]
        k = raw[:, channels + h * 64 : channels + (h + 1) * 64]
        v = raw[:, 2 * channels + h * 64 : 2 * channels + (h + 1) * 64].astype(BF)
        q = q * lax.rsqrt(jnp.sum(q * q, axis=-1, keepdims=True) + eps_unit)
        k = k * lax.rsqrt(jnp.sum(k * k, axis=-1, keepdims=True) + eps_unit)
        scores = dot_nt(q.astype(BF), k.astype(BF))
        weights = jnp.exp(scores * scale_ref[h])
        total = jnp.sum(weights, axis=-1, keepdims=True)
        mixed.append(dot(weights.astype(BF), v) / total)
    mixed = jnp.concatenate(mixed, axis=1).astype(BF)
    normed, _ = layer_norm(dot(mixed, proj_ref[...]))
    stream = (x.astype(F32) + normed).astype(BF)
    own = stream.shape[0] // 4
    for k in range(4):
        out_ref[:, k * channels : (k + 1) * channels] = stream[k * own : (k + 1) * own]
        cot_ref[k * 16 : (k + 1) * 16, :channels] = quads[k][64:80]
        cot_ref[k * 16 : (k + 1) * 16, channels:] = quads[k][80:]


def level_kernel(merged_ref, own_ref, core_ref, near_ref, far_ref, level_ref, bf_ref):
    merged = merged_ref[...]
    parts = [dot_nt(merged, r[...]) for r in (own_ref, core_ref, near_ref, far_ref)]
    xl, core = lax.axis_index("xl") == 0, lax.axis_index("core") == 0
    low = [jnp.where(xl, parts[k], parts[k + 2]) for k in (0, 1)]
    high = [jnp.where(xl, parts[k + 2], parts[k]) for k in (0, 1)]
    ordered = []
    for pair in (low, high):
        ordered += [jnp.where(core, pair[0], pair[1]), jnp.where(core, pair[1], pair[0])]
    level, _ = layer_norm(jnp.concatenate(ordered, axis=1))
    level_ref[...] = level
    bf_ref[...] = level.astype(BF)


def whole(count):
    return [pl.BlockSpec(memory_space=pltpu.VMEM)] * count


def whole_step(fields, logit_scale, w_qkv, w_proj, w_merge, w_up, w_down, cotangent):
    tile_rows, tile_cols, channels = fields.shape
    wide = cotangent.shape[-1]
    tokens = tile_rows * tile_cols
    own = tokens // 4

    tile_quads = pl.pallas_call(
        order_kernel,
        out_shape=[vmem((96, channels), BF)] * 4,
        in_specs=whole(2),
        out_specs=whole(4),
        compiler_params=pltpu.CompilerParams(vmem_limit_bytes=LIMIT),
        name="order",
    )(fields.reshape(tokens, channels), cotangent.reshape(own, wide))

    def to_window(quads):
        return (
            quads[3],
            to_grid(quads[2], 0, -1),
            to_grid(quads[1], -1, 0),
            to_grid(quads[0], -1, -1),
        )

    def to_tile(quads):
        return (
            to_grid(quads[3], 1, 1),
            to_grid(quads[2], 1, 0),
            to_grid(quads[1], 0, 1),
            quads[0],
        )

    x = to_window(tile_quads)

    weights = gather_rows(jnp.stack([w_up, w_down.T]))
    merge_own = w_merge.T
    merge_near = swap_xl(merge_own)
    merge_core = swap_core(merge_own)
    merge_far = swap_core(merge_near)

    merged, cot = pl.pallas_call(
        window_kernel,
        out_shape=[
            vmem((own, 4 * channels), BF),
            vmem((own, wide), BF),
        ],
        in_specs=[pl.BlockSpec(memory_space=pltpu.SMEM)] + whole(6),
        out_specs=whole(2),
        cost_estimate=pl.CostEstimate(
            flops=2 * tokens * channels * (4 * channels + 2 * tokens),
            transcendentals=tokens * tokens * 6,
            bytes_accessed=2_000_000,
        ),
        compiler_params=pltpu.CompilerParams(vmem_limit_bytes=LIMIT),
        name="window",
    )(
        logit_scale,
        *(in_vmem(q) for q in x),
        in_vmem(w_qkv),
        in_vmem(w_proj),
    )
    level, level_own = pl.pallas_call(
        level_kernel,
        out_shape=[vmem((own, wide), F32), vmem((own, wide), BF)],
        in_specs=whole(5),
        out_specs=whole(2),
        cost_estimate=pl.CostEstimate(
            flops=8 * own * channels * wide, transcendentals=own, bytes_accessed=3_000_000
        ),
        compiler_params=pltpu.CompilerParams(vmem_limit_bytes=LIMIT),
        name="level",
    )(in_vmem(merged), *(in_vmem(w) for w in (merge_own, merge_core, merge_near, merge_far)))
    level_near = swap_xl(level_own)
    level_across = swap_core(jnp.concatenate([level_own, level_near], axis=0))
    hid = w_up.shape[1]
    level_b, up_full, down_full, hidden, gelu_slope, low, high = pl.pallas_call(
        forward_kernel,
        out_shape=[
            vmem((tokens, wide), BF),
            vmem((wide, hid), BF),
            vmem((wide, hid), BF),
            vmem((tokens, hid), BF),
            vmem((tokens, hid), F32),
            vmem((2 * own, wide), BF),
            vmem((2 * own, wide), BF),
        ],
        in_specs=whole(12),
        out_specs=whole(7),
        cost_estimate=pl.CostEstimate(
            flops=4 * tokens * wide * hid, transcendentals=2 * tokens * hid, bytes_accessed=6_000_000
        ),
        compiler_params=pltpu.CompilerParams(vmem_limit_bytes=LIMIT),
        name="forward",
    )(*(in_vmem(v) for v in (level_own, level_near, level_across, *weights)))

    branch_norm, branch_inv = layer_norm(scatter_cols(low, high))
    coarse = level + branch_norm
    upstream = cot.astype(F32)
    slope_own = norm_slope(upstream, branch_norm, branch_inv).astype(BF)
    slope_near = swap_xl(slope_own)
    slope_across = swap_core(jnp.concatenate([slope_own, slope_near], axis=0))
    terms, low, high = pl.pallas_call(
        backward_kernel,
        out_shape=[
            vmem((NZ, NX, 2, w_up.shape[0], hid), BF),
            vmem((2 * own, wide), BF),
            vmem((2 * own, wide), BF),
        ],
        in_specs=whole(8),
        out_specs=whole(3),
        scratch_shapes=[pltpu.VMEM((tokens, wide), BF)],
        cost_estimate=pl.CostEstimate(
            flops=8 * tokens * wide * hid, transcendentals=0, bytes_accessed=6_000_000
        ),
        compiler_params=pltpu.CompilerParams(vmem_limit_bytes=LIMIT),
        name="backward",
    )(
        *(
            in_vmem(v)
            for v in (
                slope_own,
                slope_near,
                slope_across,
                level_b,
                up_full,
                down_full,
                hidden,
                gelu_slope,
            )
        )
    )
    grad_down, grad_up = scatter_rows(terms)
    grad_coarse = upstream + scatter_cols(low, high)

    both = jnp.concatenate([coarse, grad_coarse], axis=1).astype(BF)
    quads = to_tile([both[k * 16 : (k + 1) * 16] for k in range(4)])
    both = jnp.stack(quads).reshape(2, 2, 4, 4, 2 * wide).transpose(0, 2, 1, 3, 4)
    both = both.reshape(tile_rows // 2, tile_cols // 2, 2 * wide).astype(F32)
    return (both[..., :wide], both[..., wide:], grad_up, grad_down.T)


def solution(mesh):
    finer = Mesh(
        mesh.devices.reshape(NX, NZ, NL, NCORE, mesh.shape["dp"]),
        ("xh", "z", "xl", "core", "dp"),
    )
    rows = ("dp", *ROWS)
    in_specs = (
        P(rows, COLS, None),
        P(),
        P(),
        P(),
        P(None, COLS),
        P(ROWS, COLS),
        P(COLS, ROWS),
        P(rows, COLS, None),
    )
    out_specs = (
        P(rows, COLS, None),
        P(rows, COLS, None),
        P(ROWS, ("dp", *COLS)),
        P(COLS, rows),
    )
    return jax.shard_map(
        whole_step, mesh=finer, in_specs=in_specs, out_specs=out_specs, check_vma=False
    )
```

```python
import jax
import jax.numpy as jnp
from jax import lax
from jax.experimental import pallas as pl
from jax.experimental.pallas import tpu as pltpu
from jax.sharding import Mesh
from jax.sharding import PartitionSpec as P


NX, NZ, NL, NCORE = 2, 8, 2, 2
ROWS = ("xh", "z")
COLS = ("xl", "core")
GRID = ("xh", "z", "xl", "core")
NROW, NCOL = NX * NZ, NL * NCORE

eps_norm = 1e-05
eps_unit = 1e-06
BF = jnp.bfloat16
LIMIT = 24 * 2**20
F32 = jnp.float32


def dot(a, b):
    return jnp.dot(a, b, preferred_element_type=F32)


def dot_nt(a, b):
    return lax.dot_general(a, b, (((1,), (1,)), ((), ())), preferred_element_type=F32)


def dot_tn(a, b):
    return lax.dot_general(a, b, (((0,), (0,)), ((), ())), preferred_element_type=F32)


def layer_norm(value):
    average = jnp.mean(value, axis=-1, keepdims=True)
    centred = value - average
    spread = jnp.mean(centred * centred, axis=-1, keepdims=True)
    inverse = lax.rsqrt(spread + eps_norm)
    return (centred * inverse, inverse)


def norm_slope(upstream, normed, inverse):
    first_mean = jnp.mean(upstream, axis=-1, keepdims=True)
    second_mean = jnp.mean(upstream * normed, axis=-1, keepdims=True)
    return inverse * (upstream - first_mean - normed * second_mean)


def in_vmem(array):
    return pltpu.with_memory_space_constraint(array, pltpu.VMEM)


def vmem(shape, dtype):
    return pltpu.VMEM(shape, dtype)


def to_grid(array, dr, dc):
    pairs = [
        (r * NCOL + c, ((r + dr) % NROW) * NCOL + (c + dc) % NCOL)
        for r in range(NROW)
        for c in range(NCOL)
    ]
    return lax.ppermute(array, GRID, pairs)


def swap_core(array):
    return lax.ppermute(array, "core", [(0, 1), (1, 0)])


def swap_xl(array):
    return lax.ppermute(array, "xl", [(0, 1), (1, 0)])


def swap_half(array):
    return lax.ppermute(array, "xh", [(0, 1), (1, 0)])


def along_z(array, step):
    return lax.ppermute(array, "z", [(i, (i + step) % NZ) for i in range(NZ)])


def across_z(array, step):
    pairs = []
    for h in range(NX):
        for i in range(NZ):
            pairs.append((h * NZ + i, (1 - h) * NZ + (i + step) % NZ))
    return lax.ppermute(array, ROWS, pairs)


def scatter_cols(low, high):
    quarter = low.shape[0] // 2
    near = low.astype(F32) + swap_core(high).astype(F32)
    far = swap_xl(near[quarter:].astype(BF))
    return near[:quarter] + far.astype(F32)


def gather_rows(shard):
    other = swap_half(shard)
    own = pl.pallas_call(
        pair_kernel,
        out_shape=vmem((NX, *shard.shape), shard.dtype),
        in_specs=whole(2),
        out_specs=whole(1)[0],
        compiler_params=pltpu.CompilerParams(vmem_limit_bytes=LIMIT),
        name="pair",
    )(in_vmem(shard), in_vmem(other))
    pieces = [own]
    left = right = own
    for _ in range(3):
        left, right = along_z(left, -1), along_z(right, 1)
        pieces += [left, right]
    far = [along_z(left[0], -1), along_z(right[1], 1)]
    return pieces + far


def scatter_rows(terms):
    apart = lax.optimization_barrier(terms)

    def block(k):
        return (terms if k < 5 else apart)[k]

    own, far = block(0), block(4)
    own_other = swap_half(own[1])
    left, right = along_z(far[0], -1), along_z(far[1], 1)
    near_left, near_right = block(NZ - 3), block(3)
    left = jnp.stack([near_left[0] + left, near_left[1]])
    right = jnp.stack([near_right[0], near_right[1] + right])
    for k in (2, 1):
        left = along_z(left, -1)
        right = along_z(right, 1)
        left, right = left + block(NZ - k), right + block(k)
    near, cross = [along_z(left[0], -1)], [across_z(left[1], -1)]
    near, cross = near + [along_z(right[0], 1)], cross + [across_z(right[1], 1)]
    shape = jax.ShapeDtypeStruct(own.shape[2:], F32)
    return pl.pallas_call(
        finish_kernel,
        out_shape=[shape] * 2,
        in_specs=whole(6),
        out_specs=whole(2),
        compiler_params=pltpu.CompilerParams(vmem_limit_bytes=LIMIT),
        name="finish",
    )(*(in_vmem(v) for v in (own[0], own_other, *near, *cross)))


def pair_kernel(own_ref, other_ref, out_ref):
    first = lax.axis_index("xh") == 0
    out_ref[0] = jnp.where(first, own_ref[...], other_ref[...])
    out_ref[1] = jnp.where(first, other_ref[...], own_ref[...])


def forward_kernel(*refs):
    level, near, across = refs[:3]
    pieces = refs[3:10]
    far = refs[10:12]
    level_b, up, down, hidden_ref, slope_ref, low_ref, high_ref = refs[12:]
    own = level.shape[0]
    level_b[:own] = level[...]
    level_b[own : 2 * own] = near[...]
    level_b[2 * own :] = across[...]
    z = lax.axis_index("z")
    rows = pieces[0].shape[2]

    def put(piece, half, k):
        start = pl.multiple_of((half * NZ + lax.rem(z + k, NZ)) * rows, 16)
        up[pl.ds(start, rows), :] = piece[0]
        down[pl.ds(start, rows), :] = piece[1]

    for piece, k in zip(pieces, (0, 1, 7, 2, 6, 3, 5)):
        for half in (0, 1):
            put(piece[half], half, k)
    put(far[0][...], 0, 4)
    put(far[1][...], 1, 4)
    pre = dot(level_b[...], up[...])
    share = 0.5 + 0.5 * lax.erf(pre * 0.7071067811865476)
    slope_ref[...] = share + pre * (0.3989422804014327 * jnp.exp(-0.5 * pre * pre))
    hidden = (pre * share).astype(BF)
    hidden_ref[...] = hidden
    sums = dot_nt(hidden, down[...]).astype(BF)
    low_ref[...] = sums[: 2 * own]
    high_ref[...] = sums[2 * own :]


def backward_kernel(*refs):
    own_ref, near, across, level_b, up, down, hidden, gelu_slope = refs[:8]
    terms, low_ref, high_ref, slope = refs[8:]
    own = own_ref.shape[0]
    slope[:own] = own_ref[...]
    slope[own : 2 * own] = near[...]
    slope[2 * own :] = across[...]
    z, xh = lax.axis_index("z"), lax.axis_index("xh")
    rows = terms.shape[3]

    def put(term, which):
        for half in range(NX):
            for at in range(NZ):
                start = (half * NZ + at) * rows
                block = term[start : start + rows]
                terms[lax.rem(at + NZ - z, NZ), lax.rem(half + xh, NX), which] = block

    put(dot_tn(slope[...], hidden[...]).astype(BF), 0)
    pre = (gelu_slope[...] * dot(slope[...], down[...])).astype(BF)
    put(dot_tn(level_b[...], pre).astype(BF), 1)
    sums = dot_nt(pre, up[...]).astype(BF)
    low_ref[...] = sums[: 2 * own]
    high_ref[...] = sums[2 * own :]


def finish_kernel(*refs):
    total = refs[0][...].astype(F32)
    for part in refs[1:-2]:
        total = total + part[...].astype(F32)
    refs[-2][...] = total[0]
    refs[-1][...] = total[1]


def order_kernel(fields_ref, cot_ref, *outs):
    n = fields_ref.shape[0]
    to = lax.broadcasted_iota(jnp.int32, (n, n), 0)
    at = lax.broadcasted_iota(jnp.int32, (n, n), 1)
    c4, r4 = to & 3, (to >> 2) & 3
    pr, pc = (to >> 4) & 1, (to >> 5) & 1
    qb, qa = (to >> 6) & 1, (to >> 7) & 1
    source = (qa * 8 + r4 * 2 + pr) * 16 + qb * 8 + c4 * 2 + pc
    pick = jnp.where(at == source, 1.0, 0.0).astype(BF)
    moved = dot(pick, fields_ref[...].astype(BF)).astype(BF)
    m = cot_ref.shape[0]
    to = lax.broadcasted_iota(jnp.int32, (m, m), 0)
    at = lax.broadcasted_iota(jnp.int32, (m, m), 1)
    source = (((to >> 5) & 1) * 4 + ((to >> 2) & 3)) * 8 + ((to >> 4) & 1) * 4 + (to & 3)
    pick = jnp.where(at == source, 1.0, 0.0).astype(BF)
    cot = dot(pick, cot_ref[...]).astype(BF)
    wide = fields_ref.shape[1]
    for k in range(4):
        outs[k][:64] = moved[k * 64 : (k + 1) * 64]
        outs[k][64:80] = cot[k * 16 : (k + 1) * 16, :wide]
        outs[k][80:] = cot[k * 16 : (k + 1) * 16, wide:]


def window_kernel(scale_ref, x0, x1, x2, x3, qkv_ref, proj_ref, out_ref, cot_ref):
    quads = (x0[...], x1[...], x2[...], x3[...])
    x = jnp.concatenate([q[k * 16 : (k + 1) * 16] for k in range(4) for q in quads], axis=0)
    channels = x.shape[1]
    heads = channels // 64
    raw = dot(x, qkv_ref[...])
    mixed = []
    for h in range(heads):
        q = raw[:, h * 64 : (h + 1) * 64]
        k = raw[:, channels + h * 64 : channels + (h + 1) * 64]
        v = raw[:, 2 * channels + h * 64 : 2 * channels + (h + 1) * 64].astype(BF)
        q = q * lax.rsqrt(jnp.sum(q * q, axis=-1, keepdims=True) + eps_unit)
        k = k * lax.rsqrt(jnp.sum(k * k, axis=-1, keepdims=True) + eps_unit)
        scores = dot_nt(q.astype(BF), k.astype(BF))
        weights = jnp.exp(scores * scale_ref[h])
        total = jnp.sum(weights, axis=-1, keepdims=True)
        mixed.append(dot(weights.astype(BF), v) / total)
    mixed = jnp.concatenate(mixed, axis=1).astype(BF)
    normed, _ = layer_norm(dot(mixed, proj_ref[...]))
    stream = (x.astype(F32) + normed).astype(BF)
    own = stream.shape[0] // 4
    for k in range(4):
        out_ref[:, k * channels : (k + 1) * channels] = stream[k * own : (k + 1) * own]
        cot_ref[k * 16 : (k + 1) * 16, :channels] = quads[k][64:80]
        cot_ref[k * 16 : (k + 1) * 16, channels:] = quads[k][80:]


def level_kernel(merged_ref, own_ref, core_ref, near_ref, far_ref, level_ref, bf_ref):
    merged = merged_ref[...]
    parts = [dot_nt(merged, r[...]) for r in (own_ref, core_ref, near_ref, far_ref)]
    xl, core = lax.axis_index("xl") == 0, lax.axis_index("core") == 0
    low = [jnp.where(xl, parts[k], parts[k + 2]) for k in (0, 1)]
    high = [jnp.where(xl, parts[k + 2], parts[k]) for k in (0, 1)]
    ordered = []
    for pair in (low, high):
        ordered += [jnp.where(core, pair[0], pair[1]), jnp.where(core, pair[1], pair[0])]
    level, _ = layer_norm(jnp.concatenate(ordered, axis=1))
    level_ref[...] = level
    bf_ref[...] = level.astype(BF)


def whole(count):
    return [pl.BlockSpec(memory_space=pltpu.VMEM)] * count


def whole_step(fields, logit_scale, w_qkv, w_proj, w_merge, w_up, w_down, cotangent):
    tile_rows, tile_cols, channels = fields.shape
    wide = cotangent.shape[-1]
    tokens = tile_rows * tile_cols
    own = tokens // 4

    tile_quads = pl.pallas_call(
        order_kernel,
        out_shape=[vmem((96, channels), BF)] * 4,
        in_specs=whole(2),
        out_specs=whole(4),
        compiler_params=pltpu.CompilerParams(vmem_limit_bytes=LIMIT),
        name="order",
    )(fields.reshape(tokens, channels), cotangent.reshape(own, wide))

    def to_window(quads):
        return (
            quads[3],
            to_grid(quads[2], 0, -1),
            to_grid(quads[1], -1, 0),
            to_grid(quads[0], -1, -1),
        )

    def to_tile(quads):
        return (
            to_grid(quads[3], 1, 1),
            to_grid(quads[2], 1, 0),
            to_grid(quads[1], 0, 1),
            quads[0],
        )

    x = to_window(tile_quads)

    weights = gather_rows(jnp.stack([w_up, w_down.T]))
    merge_own = w_merge.T
    merge_near = swap_xl(merge_own)
    merge_core = swap_core(merge_own)
    merge_far = swap_core(merge_near)

    merged, cot = pl.pallas_call(
        window_kernel,
        out_shape=[
            vmem((own, 4 * channels), BF),
            vmem((own, wide), BF),
        ],
        in_specs=[pl.BlockSpec(memory_space=pltpu.SMEM)] + whole(6),
        out_specs=whole(2),
        cost_estimate=pl.CostEstimate(
            flops=2 * tokens * channels * (4 * channels + 2 * tokens),
            transcendentals=tokens * tokens * 6,
            bytes_accessed=2_000_000,
        ),
        compiler_params=pltpu.CompilerParams(vmem_limit_bytes=LIMIT),
        name="window",
    )(
        logit_scale,
        *(in_vmem(q) for q in x),
        in_vmem(w_qkv),
        in_vmem(w_proj),
    )
    level, level_own = pl.pallas_call(
        level_kernel,
        out_shape=[vmem((own, wide), F32), vmem((own, wide), BF)],
        in_specs=whole(5),
        out_specs=whole(2),
        cost_estimate=pl.CostEstimate(
            flops=8 * own * channels * wide, transcendentals=own, bytes_accessed=3_000_000
        ),
        compiler_params=pltpu.CompilerParams(vmem_limit_bytes=LIMIT),
        name="level",
    )(in_vmem(merged), *(in_vmem(w) for w in (merge_own, merge_core, merge_near, merge_far)))
    level_near = swap_xl(level_own)
    level_across = swap_core(jnp.concatenate([level_own, level_near], axis=0))
    hid = w_up.shape[1]
    level_b, up_full, down_full, hidden, gelu_slope, low, high = pl.pallas_call(
        forward_kernel,
        out_shape=[
            vmem((tokens, wide), BF),
            vmem((wide, hid), BF),
            vmem((wide, hid), BF),
            vmem((tokens, hid), BF),
            vmem((tokens, hid), F32),
            vmem((2 * own, wide), BF),
            vmem((2 * own, wide), BF),
        ],
        in_specs=whole(12),
        out_specs=whole(7),
        cost_estimate=pl.CostEstimate(
            flops=4 * tokens * wide * hid, transcendentals=2 * tokens * hid, bytes_accessed=6_000_000
        ),
        compiler_params=pltpu.CompilerParams(vmem_limit_bytes=LIMIT),
        name="forward",
    )(*(in_vmem(v) for v in (level_own, level_near, level_across, *weights)))

    branch_norm, branch_inv = layer_norm(scatter_cols(low, high))
    coarse = level + branch_norm
    upstream = cot.astype(F32)
    slope_own = norm_slope(upstream, branch_norm, branch_inv).astype(BF)
    slope_near = swap_xl(slope_own)
    slope_across = swap_core(jnp.concatenate([slope_own, slope_near], axis=0))
    terms, low, high = pl.pallas_call(
        backward_kernel,
        out_shape=[
            vmem((NZ, NX, 2, w_up.shape[0], hid), BF),
            vmem((2 * own, wide), BF),
            vmem((2 * own, wide), BF),
        ],
        in_specs=whole(8),
        out_specs=whole(3),
        scratch_shapes=[pltpu.VMEM((tokens, wide), BF)],
        cost_estimate=pl.CostEstimate(
            flops=8 * tokens * wide * hid, transcendentals=0, bytes_accessed=6_000_000
        ),
        compiler_params=pltpu.CompilerParams(vmem_limit_bytes=LIMIT),
        name="backward",
    )(
        *(
            in_vmem(v)
            for v in (
                slope_own,
                slope_near,
                slope_across,
                level_b,
                up_full,
                down_full,
                hidden,
                gelu_slope,
            )
        )
    )
    grad_down, grad_up = scatter_rows(terms)
    grad_coarse = upstream + scatter_cols(low, high)

    both = jnp.concatenate([coarse, grad_coarse], axis=1).astype(BF)
    quads = to_tile([both[k * 16 : (k + 1) * 16] for k in range(4)])
    both = jnp.stack(quads).reshape(2, 2, 4, 4, 2 * wide).transpose(0, 2, 1, 3, 4)
    both = both.reshape(tile_rows // 2, tile_cols // 2, 2 * wide).astype(F32)
    return (both[..., :wide], both[..., wide:], grad_up, grad_down.T)


def solution(mesh):
    finer = Mesh(
        mesh.devices.reshape(NX, NZ, NL, NCORE, mesh.shape["dp"]),
        ("xh", "z", "xl", "core", "dp"),
    )
    rows = ("dp", *ROWS)
    in_specs = (
        P(rows, COLS, None),
        P(),
        P(),
        P(),
        P(None, COLS),
        P(ROWS, COLS),
        P(COLS, ROWS),
        P(rows, COLS, None),
    )
    out_specs = (
        P(rows, COLS, None),
        P(rows, COLS, None),
        P(ROWS, ("dp", *COLS)),
        P(COLS, rows),
    )
    return jax.shard_map(
        whole_step, mesh=finer, in_specs=in_specs, out_specs=out_specs, check_vma=False
    )
```
